128 devices in a mesh: tm: 32 (over z, y, core), ep: 4 (over x).
Axes of the slice: x: 4, y: 4, z: 4, core: 2. Of those that a mesh axis runs over, the one named last changes fastest.
Arguments:
- queries: bfloat16 [16384, 1024], P(('tm', 'ep')), may hold values from -256 to 256
- keys: bfloat16 [16384, 1024], P(('tm', 'ep')), may hold values from -6 to 6
- values: bfloat16 [16384, 1024], P(('tm', 'ep')), may hold values from -6 to 6
- stream: bfloat16 [16384, 1024], P(('tm', 'ep')), may hold values from -16 to 16
- grad_out: bfloat16 [16384, 1024], P(('tm', 'ep')), may hold values from -6 to 6
- norm_gain: float32 [1024], replicated, may hold values from 0.1 to 1.9
- gate_probs: float32 [16384, 2], P(('tm', 'ep')), may hold values from 0.1 to 0.9
- routes: int32 [16384, 2], P(('tm', 'ep')), may hold values from 0 to 31, all different within a row; in each aligned block of 128 rows (0 to 127, 128 to 255, ...) at most 12 rows name the same one
- w_gate: bfloat16 [32, 1024, 4096], P('tm', None, 'ep'), may hold values from -0.1875 to 0.1875
- w_up: bfloat16 [32, 1024, 4096], P('tm', None, 'ep'), may hold values from -0.1875 to 0.1875
- w_down: bfloat16 [32, 4096, 1024], P('tm', 'ep'), may hold values from -0.09375 to 0.09375
Outputs:
- queries_grad: bfloat16 [16384, 1024], P(('tm', 'ep'))
- keys_grad: bfloat16 [16384, 1024], P(('tm', 'ep'))
- values_grad: bfloat16 [16384, 1024], P(('tm', 'ep'))
- stream_grad: bfloat16 [16384, 1024], P(('tm', 'ep'))
- gate_weight_grad: float32 [32, 1024, 4096], P('tm', None, 'ep')
- up_weight_grad: float32 [32, 1024, 4096], P('tm', None, 'ep')
- down_weight_grad: float32 [32, 4096, 1024], P('tm', 'ep')
The draws below stay inside these ranges and needn't reach their ends.
Inputs may be any that keep to these rules, and one draw needn't show every extreme that they name: `routes`: in the frames of one device no expert is named by more than 12 frames, a bound that some block reaches.
All inputs are finite; a program needn't handle non-finite values.
Results may differ from the reference program's by a relative error of at most 0.015.
Values may be sent and summed in bfloat16 or wider, within the bound.
No kernel may reach another device: no remote copies, remote signals or barrier semaphores. Data moves between devices by JAX's collectives and lax.ppermute only.
A program may use at most 128 MiB of HBM per device.

```python
import math
import jax
import jax.numpy as jnp
import numpy as np
from jax import lax

D = 1024
HEADS = 16
HEAD = 64
HID = 4096
TOPK = 2
SPAN = 64
LEFT = 256
FR_DEV = 128
EXPERTS = 32
FRAMES = 16384
CAP = 12
N_TM = 32
N_EP = 4


def attention_pair(key):
    base_key = jax.random.fold_in(key, 4711)
    keys_base = jnp.clip(jax.random.normal(jax.random.fold_in(base_key, 1), (FRAMES, D), jnp.float32), -6.0, 6.0)
    queries_base = jnp.clip(jax.random.normal(jax.random.fold_in(base_key, 2), (FRAMES, D), jnp.float32), -6.0, 6.0)
    return (queries_base, keys_base)


def draw_queries(key, part):
    query_out, key_out = attention_pair(key)
    return query_out.astype(jnp.bfloat16)


def draw_keys(key, part):
    query_out, key_out = attention_pair(key)
    return key_out.astype(jnp.bfloat16)


def draw_stream(key, part):
    base_key = jax.random.fold_in(key, 913)
    column_scale = jnp.exp(jax.random.uniform(jax.random.fold_in(base_key, 1), (1, D), minval=math.log(0.3), maxval=math.log(3.0)))
    row_scale = jnp.exp(jax.random.uniform(jax.random.fold_in(base_key, 2), (FRAMES, 1), minval=math.log(0.1), maxval=math.log(1.0)))
    core_vals = jnp.clip(jax.random.normal(jax.random.fold_in(base_key, 4), (FRAMES, D), jnp.float32), -5.0, 5.0)
    return (core_vals * row_scale * column_scale).astype(jnp.bfloat16)


def steps_of(own_key, dims, shards, smallest, high):
    gain, own = 1.0, jax.random.fold_in(own_key, 6)
    for position, shards_of in shards:
        steps = jnp.exp(jax.random.uniform(jax.random.fold_in(own, position), (shards_of,), jnp.float32, smallest / len(shards), high / len(shards)))
        gain = gain * jnp.repeat(steps, dims[position] // shards_of).reshape([-1 if axis == position else 1 for axis in range(len(dims))])
    return gain


def routed_block(stream_key, own, number, rows, count, top, reach, skew):
    ranking = jax.random.permutation(stream_key, count)
    packed, ordinary = shares(count, rows * top, reach, skew, True), shares(count, rows * top, reach, skew, False)
    places = jnp.arange(count)

    def named(sizes, turn):
        used = int((sizes > 0).sum())
        fixed = max(1, used // 4)
        passed = fixed + (places - fixed + turn * (used - fixed)) % max(1, count - fixed)
        return jnp.zeros((count,), jnp.int32).at[ranking[jnp.where(places < fixed, places, passed)]].set(jnp.asarray(sizes, jnp.int32))

    sizes = jnp.where(number % 4 == 0, named(packed, number // 4), named(ordinary, number - number // 4 - 1))
    mixed = jax.random.permutation(jax.random.fold_in(own, 3), count)
    source_of, sink = mixed[0:count // 2 * 2:2], mixed[1:count // 2 * 2:2]
    room = jnp.minimum(sizes[source_of] - 1, reach - sizes[sink]) // 2
    room = jnp.where((source_of == ranking[0]) | (sink == ranking[0]) | (sizes[sink] == 0), 0, jnp.maximum(room, 0))
    passed = jax.random.randint(jax.random.fold_in(own, 4), (count // 2,), 0, 1 << 20) % (room + 1)
    sizes = sizes.at[source_of].add(-passed).at[sink].add(passed)
    items = jnp.searchsorted(jnp.cumsum(sizes), jnp.arange(rows * top), side="right").astype(jnp.int32)
    listing = items.reshape(top, rows).T
    listing = listing[jax.random.permutation(jax.random.fold_in(own, 1), rows)]
    turn = jax.random.randint(jax.random.fold_in(own, 2), (rows, 1), 0, top)
    return jnp.take_along_axis(listing, (jnp.arange(top)[None, :] + turn) % top, axis=1)


def shares(number_of, total, bound, skew, full):
    loads = [(1 << 20) // math.isqrt(grade ** skew) + 1 for grade in range(1, number_of + 1)]
    largest = bound if full else min(bound, max(-(-total // number_of), total * loads[0] // sum(loads)))
    least = 1 if total - largest >= number_of - 1 else 0
    counts, spare = [largest] + [least] * (number_of - 1), total - largest - least * (number_of - 1)
    while spare > 0:
        free = [i for i in range(1, number_of) if counts[i] < largest] or [i for i in range(1, number_of) if counts[i] < bound]
        whole, remaining = sum([loads[i] for i in free]), spare
        for i in free:
            addition = min(bound - counts[i], max(1, remaining * loads[i] // whole), spare)
            counts[i] = counts[i] + addition
            spare = spare - addition
    return np.array(counts)


def scatter_about(own_key, extent, scale, bound, cuts=(), kind=jnp.bfloat16):
    drawn = scale * jax.random.normal(own_key, extent, jnp.float32)
    if cuts:
        drawn = drawn * steps_of(own_key, extent, cuts, -0.22, 0.18)
    return jnp.clip(drawn, -bound, bound).astype(kind)


def setup_inputs(seed: int = 0) -> dict:
    streams_of = jax.random.split(jax.random.key(seed), 12)
    queries = draw_queries(jax.random.fold_in(streams_of[11], 71), 0)
    keys = draw_keys(jax.random.fold_in(streams_of[11], 71), 0)
    values = scatter_about(streams_of[2], (FRAMES, D), 1.0, 6.0, ((0, 128),))
    stream = draw_stream(jax.random.fold_in(streams_of[11], 71), 0)
    grad_out = scatter_about(streams_of[4], (FRAMES, D), 1.0, 6.0, ((0, 128),))
    norm_gain = jnp.clip(1.0 + 0.18 * jax.random.normal(streams_of[5], (D,), jnp.float32), 0.1, 1.9)
    gate_probs = jnp.clip(0.1 + 0.79999997 * jax.random.uniform(streams_of[6], (FRAMES, TOPK), jnp.float32) ** steps_of(streams_of[6], (FRAMES, TOPK), ((0, 128),), -0.2, 0.2), 0.1, 0.9)
    routes_keys = jax.random.split(jax.random.fold_in(streams_of[7], 1), FRAMES // FR_DEV)
    routes_turns = jax.random.permutation(jax.random.fold_in(streams_of[7], 3), FRAMES // FR_DEV)
    routes = jax.vmap(lambda own, number: routed_block(jax.random.fold_in(streams_of[7], 2), own, number, FR_DEV, EXPERTS, TOPK, CAP, 2))(routes_keys, routes_turns).reshape((FRAMES, TOPK))
    w_gate = scatter_about(streams_of[8], (EXPERTS, D, HID), D ** -0.5, 0.1875, ((0, 32), (2, 4)))
    w_up = scatter_about(streams_of[9], (EXPERTS, D, HID), D ** -0.5, 0.1875, ((0, 32), (2, 4)))
    w_down = scatter_about(streams_of[10], (EXPERTS, HID, D), HID ** -0.5, 0.09375, ((0, 32), (1, 4)))
    return {"queries": queries, "keys": keys, "values": values, "stream": stream, "grad_out": grad_out, "norm_gain": norm_gain, "gate_probs": gate_probs, "routes": routes, "w_gate": w_gate, "w_up": w_up, "w_down": w_down}


EPSILON = 1e-06
HIGHEST = lax.Precision.HIGHEST

def expert_grads(xin, gin, weight_gate, weight_up, weight_down):
    gate_pre = jnp.dot(xin, weight_gate, preferred_element_type=jnp.float32)
    up_pre = jnp.dot(xin, weight_up, preferred_element_type=jnp.float32)
    sigmoid_g = jax.nn.sigmoid(gate_pre)
    silu_g = gate_pre * sigmoid_g
    acted = (silu_g * up_pre).astype(jnp.bfloat16)
    dact = jnp.dot(gin, weight_down.T, preferred_element_type=jnp.float32)
    down_grad = jnp.dot(acted.T, gin, preferred_element_type=jnp.float32)
    dgate = (dact * up_pre * sigmoid_g * (1.0 + gate_pre * (1.0 - sigmoid_g))).astype(jnp.bfloat16)
    dup = (dact * silu_g).astype(jnp.bfloat16)
    gate_grad = jnp.dot(xin.T, dgate, preferred_element_type=jnp.float32)
    up_grad = jnp.dot(xin.T, dup, preferred_element_type=jnp.float32)
    dxin = jnp.dot(dgate, weight_gate.T, preferred_element_type=jnp.float32) + jnp.dot(dup, weight_up.T, preferred_element_type=jnp.float32)
    return (dxin, gate_grad, up_grad, down_grad)

def attend_grads(query_rows, key_rows, value_rows, grad_rows, allowed):
    n_query = query_rows.shape[0]
    n_key = key_rows.shape[0]
    score_scale = 1.0 / math.sqrt(HEAD)
    q_three = query_rows.astype(jnp.float32).reshape(n_query, HEADS, HEAD)
    k_three = key_rows.astype(jnp.float32).reshape(n_key, HEADS, HEAD)
    v_three = value_rows.astype(jnp.float32).reshape(n_key, HEADS, HEAD)
    o_three = grad_rows.astype(jnp.float32).reshape(n_query, HEADS, HEAD)
    scores = jnp.einsum('qhd,khd->hqk', q_three, k_three, precision=HIGHEST) * score_scale
    scores = jnp.where(allowed[None], scores, -jnp.inf)
    row_max = lax.optimization_barrier(jnp.max(scores, -1, keepdims=True))
    exp_scores = jnp.exp(scores - row_max)
    probabilities = exp_scores / lax.optimization_barrier(jnp.sum(exp_scores, -1, keepdims=True))
    pround = probabilities.astype(jnp.bfloat16).astype(jnp.float32)
    attn = jnp.einsum('hqk,khd->qhd', pround, v_three, precision=HIGHEST)
    row_delta = lax.optimization_barrier(jnp.sum(o_three * attn, -1))
    dprob = jnp.einsum('qhd,khd->hqk', o_three, v_three, precision=HIGHEST)
    dscore = (probabilities * (dprob - row_delta.T[:, :, None])).astype(jnp.bfloat16).astype(jnp.float32)
    grad_q = jnp.einsum('hqk,khd->qhd', dscore, k_three, precision=HIGHEST) * score_scale
    grad_k = jnp.einsum('hqk,qhd->khd', dscore, q_three, precision=HIGHEST) * score_scale
    grad_v = jnp.einsum('hqk,qhd->khd', pround, o_three, precision=HIGHEST)
    return (grad_q.reshape(n_query, D), grad_k.reshape(n_key, D), grad_v.reshape(n_key, D))

def reference(queries, keys, values, stream, grad_out, norm_gain, gate_probs, routes, w_gate, w_up, w_down):
    devices = N_TM * N_EP
    stream_f = stream.astype(jnp.float32)
    inverse_rms = lax.rsqrt(lax.optimization_barrier(jnp.mean(stream_f * stream_f, -1, keepdims=True)) + EPSILON)
    scaled = stream_f * inverse_rms
    normed = (scaled * norm_gain).astype(jnp.bfloat16)
    egrad = (gate_probs[:, :, None] * grad_out.astype(jnp.float32)[:, None, :]).astype(jnp.bfloat16)
    flat_routes = routes.reshape(devices, FR_DEV * TOPK)
    onehot = (flat_routes[:, :, None] == jnp.arange(EXPERTS, dtype=jnp.int32)[None, None, :]).astype(jnp.int32)
    before = jnp.cumsum(onehot, 1) - onehot
    slot_index = lax.optimization_barrier(jnp.sum(before * onehot, 2)).astype(jnp.int32)
    device_rows = (jnp.arange(devices, dtype=jnp.int32) * CAP)[:, None]
    destination = (flat_routes * (devices * CAP) + device_rows + slot_index).reshape(-1).astype(jnp.int32)
    rows_total = EXPERTS * devices * CAP
    buffer_x = jnp.zeros((rows_total, D), jnp.bfloat16).at[destination].set(jnp.repeat(normed, TOPK, axis=0))
    buffer_g = jnp.zeros((rows_total, D), jnp.bfloat16).at[destination].set(egrad.reshape(-1, D))

    def one_expert(operands):
        return expert_grads(*operands)
    dx_rows, gate_grad, up_grad, down_grad = lax.map(one_expert, (buffer_x.reshape(EXPERTS, devices * CAP, D), buffer_g.reshape(EXPERTS, devices * CAP, D), w_gate, w_up, w_down))
    dnormed = lax.optimization_barrier(jnp.sum(dx_rows.reshape(rows_total, D)[destination].reshape(FRAMES, TOPK, D), 1))
    weighted = dnormed * norm_gain
    dstream = inverse_rms * (weighted - scaled * lax.optimization_barrier(jnp.mean(weighted * scaled, -1, keepdims=True)))
    stream_grad = (grad_out.astype(jnp.float32) + dstream).astype(jnp.bfloat16)
    padded_k = jnp.concatenate([jnp.zeros((LEFT, D), jnp.bfloat16), keys], 0)
    padded_v = jnp.concatenate([jnp.zeros((LEFT, D), jnp.bfloat16), values], 0)
    window = LEFT + SPAN

    def block_step(carry, block_id):
        acc_k, acc_v = carry
        start = (block_id * SPAN).astype(jnp.int32)
        query_rows = lax.dynamic_slice_in_dim(queries, start, SPAN, 0)
        grad_rows = lax.dynamic_slice_in_dim(stream_grad, start, SPAN, 0)
        key_rows = lax.dynamic_slice_in_dim(padded_k, start, window, 0)
        value_rows = lax.dynamic_slice_in_dim(padded_v, start, window, 0)
        key_pos = start - LEFT + jnp.arange(window, dtype=jnp.int32)
        allowed = jnp.broadcast_to((key_pos >= 0)[None, :], (SPAN, window))
        grad_q, grad_k, grad_v = attend_grads(query_rows, key_rows, value_rows, grad_rows, allowed)
        old_k = lax.dynamic_slice_in_dim(acc_k, start, window, 0)
        old_v = lax.dynamic_slice_in_dim(acc_v, start, window, 0)
        acc_k = lax.dynamic_update_slice_in_dim(acc_k, old_k + grad_k, start, 0)
        acc_v = lax.dynamic_update_slice_in_dim(acc_v, old_v + grad_v, start, 0)
        return ((acc_k, acc_v), grad_q.astype(jnp.bfloat16))
    start_carry = (jnp.zeros((LEFT + FRAMES, D), jnp.float32), jnp.zeros((LEFT + FRAMES, D), jnp.float32))
    (acc_k, acc_v), grad_blocks = lax.scan(block_step, start_carry, jnp.arange(FRAMES // SPAN, dtype=jnp.int32))
    queries_grad = grad_blocks.reshape(FRAMES, D)
    keys_grad = acc_k[LEFT:].astype(jnp.bfloat16)
    values_grad = acc_v[LEFT:].astype(jnp.bfloat16)
    return (queries_grad, keys_grad, values_grad, stream_grad, gate_grad, up_grad, down_grad)
```

```python
import math

import jax
import jax.numpy as jnp
from jax import lax
from jax.experimental import pallas as pl
from jax.experimental.pallas import tpu as pltpu
from jax.sharding import PartitionSpec as P

D = 1024
HEADS = 16
HEAD = 64
SPAN = 64
LEFT = 256
FRAMES = 128
EXPERTS = 32
CAP = 12
EP = 4
ROWS = EXPERTS * EP * CAP
EPSILON = 1e-06
BF16 = jnp.bfloat16
F32 = jnp.float32
NT = (((1,), (1,)), ((), ()))
TN = (((0,), (0,)), ((), ()))


def iota(shape, dim):
    return lax.broadcasted_iota(jnp.int32, shape, dim)


def ones_where(mask):
    return jnp.where(mask, 1.0, 0.0).astype(BF16)


def matmul(a, b, dims=(((1,), (0,)), ((), ()))):
    return lax.dot_general(a, b, dims, preferred_element_type=F32)


def dispatch_x_kernel(stream_ref, gain_ref, routes_ref, gates_ref, packed_ref, meta_ref):
    s = stream_ref[...].astype(F32)
    inverse_rms = lax.rsqrt(jnp.mean(s * s, -1, keepdims=True) + EPSILON)
    normed = ((s * inverse_rms) * gain_ref[...]).astype(BF16)
    routes = routes_ref[...]
    expert = iota((EXPERTS, FRAMES), 0)
    named = [expert == routes[k : k + 1, :] for k in range(2)]
    count = ones_where(jnp.logical_or(named[0], named[1]))
    earlier = ones_where(iota((FRAMES, FRAMES), 0) < iota((FRAMES, FRAMES), 1))
    before = matmul(count, earlier)
    places = []
    for k in range(2):
        slot = jnp.sum(jnp.where(named[k], before, 0.0), 0, keepdims=True)
        places.append(routes[k : k + 1, :].astype(F32) * CAP + slot)
        meta_ref[k : k + 1, :] = places[k]
        meta_ref[2 + k : 3 + k, :] = gates_ref[k : k + 1, :]
    meta_ref[4:8, :] = jnp.zeros((4, FRAMES), F32)
    row = iota((EXPERTS * 16, FRAMES), 0)
    lane = row & 15
    base = (row >> 4) * CAP

    def pick(ids, valid):
        ids = jnp.where(valid, ids, -1).astype(F32)
        return ones_where(jnp.logical_or(ids == places[0], ids == places[1]))

    main = pick(base + lane, lane < CAP)
    for j in range(3):
        last = pick(base + (lane - CAP) + 4 * j, lane >= CAP)
        cols = slice(256 * j, 256 * (j + 1))
        packed_ref[:, cols] = (matmul(main, normed[:, cols]) + matmul(last, normed[:, 768:])).astype(BF16)


def dispatch_x(stream, gain, routes, gates):
    return pl.pallas_call(
        dispatch_x_kernel,
        out_shape=(
            jax.ShapeDtypeStruct((EXPERTS * 16, 768), BF16),
            jax.ShapeDtypeStruct((8, FRAMES), F32),
        ),
        name="dispatch_x",
    )(stream, gain, routes, gates)


def row_keys(start, count, width):
    r = iota((count, width), 0) + start
    group = (r * 1366) >> 16
    rest = r - group * 48
    source = (rest * 43) >> 9
    return (group * CAP + (rest - source * CAP) + source * 512).astype(F32)


G_BLOCK = 384


def dispatch_g_kernel(*refs):
    grads, metas, out_ref, pairs, keys = refs[:4], refs[4:8], refs[8], refs[9], refs[10]

    @pl.when(pl.program_id(0) == 0)
    def _():
        for q in range(EP):
            meta = metas[q][...]
            turned = meta.T
            g = grads[q][...].astype(F32)
            for k in range(2):
                part = slice((2 * q + k) * FRAMES, (2 * q + k + 1) * FRAMES)
                pairs[part, :] = (turned[:, 2 + k : 3 + k] * g).astype(BF16)
                keys[0:1, part] = meta[k : k + 1, :] + 512.0 * q

    key = row_keys(pl.program_id(0) * G_BLOCK, G_BLOCK, FRAMES)
    chosen = jnp.concatenate(
        [ones_where(key == keys[0:1, b * FRAMES : (b + 1) * FRAMES]) for b in range(8)], 1
    )
    out_ref[...] = matmul(chosen, pairs[...]).astype(BF16)


def dispatch_g(grads, metas):
    whole = lambda shape: pl.BlockSpec(shape, lambda i: (0, 0))
    return pl.pallas_call(
        dispatch_g_kernel,
        grid=(ROWS // G_BLOCK,),
        in_specs=[whole((FRAMES, D))] * 4 + [whole((8, FRAMES))] * 4,
        out_specs=pl.BlockSpec((G_BLOCK, D), lambda i: (i, 0)),
        out_shape=jax.ShapeDtypeStruct((ROWS, D), BF16),
        scratch_shapes=[pltpu.VMEM((8 * FRAMES, D), BF16), pltpu.VMEM((8, 8 * FRAMES), F32)],
        name="dispatch_g",
    )(*grads, *metas)


M_BLOCK = 384
STEPS = ROWS // M_BLOCK
PACKED = 16 * M_BLOCK // 48


def expert_forward_kernel(
    own_ref, left_ref, right_ref, top_ref, bottom_ref, gate_ref, up_ref, x_ref, a_ref, s_ref, acted_ref, moves
):
    step = pl.program_id(0)

    @pl.when(step == 0)
    def _():
        r = iota((192, 256), 0)
        c = iota((192, 256), 1)
        group = (r * 1366) >> 16
        rest = r - group * 48
        source = (rest * 43) >> 9
        slot = rest - source * CAP
        same = jnp.logical_and((c >> 6) == source, ((c & 63) >> 4) == group)
        lane = c & 15
        moves[0] = ones_where(jnp.logical_and(same, lane == slot))
        for j in range(3):
            hit = jnp.logical_and(same, lane == CAP + slot - 4 * j)
            hit = jnp.logical_and(hit, (slot >> 2) == j)
            moves[1 + j] = ones_where(hit)

    upper = step < STEPS // 2
    far = jnp.where(upper, top_ref[...].astype(F32), bottom_ref[...].astype(F32)).astype(BF16)
    chunks = (own_ref[...], left_ref[...], right_ref[...], far)
    for half in range(M_BLOCK // 192):
        rows = slice(192 * half, 192 * (half + 1))
        packed = jnp.concatenate([c[64 * half : 64 * (half + 1), :] for c in chunks], 0)
        x_ref[rows, 0:768] = matmul(moves[0], packed).astype(BF16)
        last = matmul(moves[1], packed[:, 0:256])
        last += matmul(moves[2], packed[:, 256:512])
        last += matmul(moves[3], packed[:, 512:768])
        x_ref[rows, 768:1024] = last.astype(BF16)
    x = x_ref[...]
    gate = matmul(x, gate_ref[...])
    up = matmul(x, up_ref[...])
    sig = jax.nn.sigmoid(gate)
    silu = gate * sig
    acted_ref[...] = (silu * up).astype(BF16)
    s_ref[...] = silu
    a_ref[...] = up * sig * (1.0 + gate * (1.0 - sig))


def expert_forward(own, left, right, top, bottom, w_gate, w_up):
    half = STEPS // 2
    rows = lambda f: pl.BlockSpec((PACKED, 768), f)
    weight = pl.BlockSpec((D, D), lambda i: (0, 0), pipeline_mode=pl.Buffered(1))
    out = pl.BlockSpec((M_BLOCK, D), lambda i: (i, 0))
    shape = lambda t: jax.ShapeDtypeStruct((ROWS, D), t)
    return pl.pallas_call(
        expert_forward_kernel,
        grid=(STEPS,),
        in_specs=[
            rows(lambda i: (i, 0)),
            rows(lambda i: (i, 0)),
            rows(lambda i: (i, 0)),
            rows(lambda i: (jnp.minimum(i, half - 1), 0)),
            rows(lambda i: (jnp.maximum(i - half, 0), 0)),
            weight,
            weight,
        ],
        out_specs=[out] * 4,
        out_shape=(shape(BF16), shape(F32), shape(F32), shape(BF16)),
        scratch_shapes=[pltpu.VMEM((4, 192, 256), BF16)],
        name="expert_forward",
    )(own, left, right, top, bottom, w_gate, w_up)


def expert_backward_kernel(g_ref, a_ref, s_ref, gate_ref, up_ref, down_ref, dgate_ref, dup_ref, dx_ref):
    dact = matmul(g_ref[...], down_ref[...], NT)
    dgate = (dact * a_ref[...]).astype(BF16)
    dup = (dact * s_ref[...]).astype(BF16)
    dgate_ref[...] = dgate
    dup_ref[...] = dup
    dx_ref[...] = (matmul(dgate, gate_ref[...], NT) + matmul(dup, up_ref[...], NT)).astype(BF16)


def expert_backward(g, a, s, w_gate, w_up, w_down):
    weight = pl.BlockSpec((D, D), lambda i: (0, 0), pipeline_mode=pl.Buffered(1))
    rows = pl.BlockSpec((M_BLOCK, D), lambda i: (i, 0))
    return pl.pallas_call(
        expert_backward_kernel,
        grid=(STEPS,),
        in_specs=[rows, rows, rows, weight, weight, weight],
        out_specs=[rows] * 3,
        out_shape=(jax.ShapeDtypeStruct((ROWS, D), BF16),) * 3,
        name="expert_backward",
    )(g, a, s, w_gate, w_up, w_down)


def combine_kernel(dx_ref, m0, m1, m2, m3, own_ref, p1_ref, p2_ref, p3_ref):
    r = iota((8, ROWS), 1)
    group = (r * 1366) >> 16
    rest = r - group * 48
    source = (rest * 43) >> 9
    key = (group * CAP + (rest - source * CAP) + source * 512).astype(F32)[0:1, :]
    dx = dx_ref[...]
    for q, (meta, out) in enumerate(zip((m0, m1, m2, m3), (own_ref, p1_ref, p2_ref, p3_ref))):
        turned = meta[...].T + 512.0 * q
        chosen = ones_where(jnp.logical_or(turned[:, 0:1] == key, turned[:, 1:2] == key))
        out[...] = matmul(chosen, dx).astype(out.dtype)


def combine(dx, metas):
    part = lambda t: jax.ShapeDtypeStruct((FRAMES, D), t)
    return pl.pallas_call(
        combine_kernel,
        out_shape=(part(F32), part(BF16), part(BF16), part(BF16)),
        name="combine",
    )(dx, *metas)


WINDOW = LEFT + FRAMES


def one_head(pair, h):
    lane = iota(pair.shape, 1)
    mask = lane >= HEAD if h else lane < HEAD
    return jnp.where(mask, pair.astype(F32), 0.0).astype(BF16)


def attention_probs_kernel(first_ref, q_ref, k2_ref, k1_ref, k0_ref, p_ref):
    keys = jnp.concatenate([k2_ref[...], k1_ref[...], k0_ref[...]], 0)
    q = q_ref[...]
    s = iota((WINDOW, FRAMES), 0)
    skipped = jnp.where(iota((WINDOW, FRAMES), 1) >= SPAN, SPAN, 0)
    allowed = jnp.logical_and(s >= skipped, s < skipped + (WINDOW - SPAN))
    allowed = jnp.logical_and(allowed, s >= first_ref[0])
    for h in range(2):
        mine = one_head(q, h)
        scores = matmul(keys, mine, NT) * (1.0 / math.sqrt(HEAD))
        scores = jnp.where(allowed, scores, -jnp.inf)
        e = jnp.exp(scores - jnp.max(scores, 0, keepdims=True))
        p_ref[h] = e / jnp.sum(e, 0, keepdims=True)


def attention_probs(first, q, k2, k1, k0):
    pair = pl.BlockSpec((FRAMES, 2 * HEAD), lambda i, *_: (0, i))
    return pl.pallas_call(
        attention_probs_kernel,
        grid_spec=pltpu.PrefetchScalarGridSpec(
            num_scalar_prefetch=1,
            grid=(HEADS // 2,),
            in_specs=[pair] * 4,
            out_specs=pl.BlockSpec((2, WINDOW, FRAMES), lambda i, *_: (i, 0, 0)),
        ),
        out_shape=jax.ShapeDtypeStruct((HEADS, WINDOW, FRAMES), F32),
        name="attention_probs",
    )(first, q, k2, k1, k0)


def finish_kernel(
    own_ref, p1_ref, p2_ref, p3_ref, stream_ref, grad_ref, gain_ref,
    p_ref, q_ref, k2_ref, k1_ref, k0_ref, v2_ref, v1_ref, v0_ref,
    o_ref, dq_ref, dk_ref, dv_ref, left1_ref, left2_ref, o_scr,
):
    i = pl.program_id(0)

    @pl.when(i == 0)
    def _():
        dnormed = own_ref[...] + p1_ref[...].astype(F32) + p2_ref[...].astype(F32) + p3_ref[...].astype(F32)
        s = stream_ref[...].astype(F32)
        inverse_rms = lax.rsqrt(jnp.mean(s * s, -1, keepdims=True) + EPSILON)
        scaled = s * inverse_rms
        weighted = dnormed * gain_ref[...]
        mean = jnp.mean(weighted * scaled, -1, keepdims=True)
        o = (grad_ref[...].astype(F32) + inverse_rms * (weighted - scaled * mean)).astype(BF16)
        o_ref[...] = o
        for j in range(HEADS // 2):
            o_scr[j] = o[:, 2 * HEAD * j : 2 * HEAD * (j + 1)]

    o = o_scr[i]
    q = q_ref[...]
    keys = jnp.concatenate([k2_ref[...], k1_ref[...], k0_ref[...]], 0)
    values = jnp.concatenate([v2_ref[...], v1_ref[...], v0_ref[...]], 0)
    dq = dk = dv = None
    for h in range(2):
        o_h, q_h, k_h = one_head(o, h), one_head(q, h), one_head(keys, h)
        probs = p_ref[h]
        rounded = probs.astype(BF16)
        dprob = matmul(values, o_h, NT)
        rowdelta = jnp.sum(rounded.astype(F32) * dprob, 0, keepdims=True)
        dscore = (probs * (dprob - rowdelta)).astype(BF16)
        parts = matmul(dscore, k_h, TN), matmul(dscore, q_h), matmul(rounded, o_h)
        dq, dk, dv = parts if h == 0 else (dq + parts[0], dk + parts[1], dv + parts[2])
    scale = 1.0 / math.sqrt(HEAD)
    dk = dk * scale
    dq_ref[...] = (dq * scale).astype(BF16)
    dk_ref[...] = dk[LEFT:]
    dv_ref[...] = dv[LEFT:]
    left2_ref[0] = dk[:FRAMES].astype(BF16)
    left2_ref[1] = dv[:FRAMES].astype(BF16)
    left1_ref[0] = dk[FRAMES:LEFT].astype(BF16)
    left1_ref[1] = dv[FRAMES:LEFT].astype(BF16)


def finish(parts, stream, grad, gain, probs, q, ks, vs):
    whole = lambda n: pl.BlockSpec((n, D), lambda i: (0, 0))
    pair = pl.BlockSpec((FRAMES, 2 * HEAD), lambda i: (0, i))
    both = pl.BlockSpec((2, FRAMES, 2 * HEAD), lambda i: (0, 0, i))
    out = lambda t: jax.ShapeDtypeStruct((FRAMES, D), t)
    sent = jax.ShapeDtypeStruct((2, FRAMES, D), BF16)
    return pl.pallas_call(
        finish_kernel,
        grid=(HEADS // 2,),
        in_specs=[whole(FRAMES)] * 6
        + [whole(1), pl.BlockSpec((2, WINDOW, FRAMES), lambda i: (i, 0, 0))]
        + [pair] * 7,
        out_specs=[whole(FRAMES), pair, pair, pair, both, both],
        out_shape=(out(BF16), out(BF16), out(F32), out(F32), sent, sent),
        scratch_shapes=[pltpu.VMEM((HEADS // 2, FRAMES, 2 * HEAD), BF16)],
        name="finish",
    )(*parts, stream, grad, gain, probs, q, *ks, *vs)


def turned(x, distance):
    return lax.ppermute(x, "ep", [(i, (i + distance) % EP) for i in range(EP)])


def shifted(x, distance):
    count = lax.axis_size("tm") * lax.axis_size("ep")
    route = [(i, i + distance) for i in range(count) if 0 <= i + distance < count]
    return lax.ppermute(x, ("tm", "ep"), route)


def exchanged(x):
    return lax.all_to_all(x, "tm", split_axis=0, concat_axis=0, tiled=True)


def body(
    queries, keys, values, stream, grad_out, norm_gain, gate_probs, routes, w_gate, w_up, w_down
):
    gain = norm_gain.reshape(1, D)
    weight_gate, weight_up, weight_down = w_gate[0], w_up[0], w_down[0]
    packed, meta = dispatch_x(stream, gain, routes.T, gate_probs.T)
    grads = (grad_out, turned(grad_out, 1), turned(grad_out, -1), turned(grad_out, 2))
    metas = (meta, turned(meta, 1), turned(meta, -1), turned(meta, 2))
    own = exchanged(packed.reshape(EXPERTS, 16, 768)).reshape(EXPERTS * 16, 768)
    left, right = turned(own, 1), turned(own, -1)
    half = EXPERTS * 8
    top, bottom = turned(left[:half], 1), turned(right[half:], -1)
    g_rows = exchanged(dispatch_g(grads, metas).reshape(EXPERTS, EP * CAP, D)).reshape(ROWS, D)
    x_rows, a, s, acted = expert_forward(own, left, right, top, bottom, weight_gate, weight_up)
    dgate, dup, dx = expert_backward(g_rows, a, s, weight_gate, weight_up, weight_down)
    returned = exchanged(dx.reshape(EXPERTS, EP * CAP, D)).reshape(ROWS, D)
    gate_grad = jnp.dot(x_rows.T, dgate, preferred_element_type=F32)
    up_grad = jnp.dot(x_rows.T, dup, preferred_element_type=F32)
    down_grad = jnp.dot(acted.T, g_rows, preferred_element_type=F32)
    mine, part1, part2, part3 = combine(returned, metas)
    parts = (mine, turned(part1, -1), turned(part2, 1), turned(part3, 2))
    ks = (shifted(keys, 2), shifted(keys, 1), keys)
    vs = (shifted(values, 2), shifted(values, 1), values)
    position = lax.axis_index("tm") * lax.axis_size("ep") + lax.axis_index("ep")
    first = jnp.maximum(LEFT - position * FRAMES, 0).astype(jnp.int32).reshape(1)
    probs = attention_probs(first, queries, *ks)
    stream_grad, grad_q, own_k, own_v, left1, left2 = finish(
        parts, stream, grad_out, gain, probs, queries, ks, vs
    )
    back1, back2 = shifted(left1, -1), shifted(left2, -2)
    back = back1.astype(F32) + back2.astype(F32)
    return (
        grad_q,
        (own_k + back[0]).astype(BF16),
        (own_v + back[1]).astype(BF16),
        stream_grad,
        gate_grad[None],
        up_grad[None],
        down_grad[None],
    )


def solution(mesh):
    frames = P(("tm", "ep"), None)
    columns, rows = P("tm", None, "ep"), P("tm", "ep", None)
    return jax.shard_map(
        body,
        mesh=mesh,
        in_specs=(frames,) * 5 + (P(), frames, frames, columns, columns, rows),
        out_specs=(frames,) * 4 + (columns, columns, rows),
        check_vma=False,
    )
```

```python
import math

import jax
import jax.numpy as jnp
from jax import lax
from jax.experimental import pallas as pl
from jax.experimental.pallas import tpu as pltpu
from jax.sharding import PartitionSpec as P

D = 1024
HEADS = 16
HEAD = 64
SPAN = 64
LEFT = 256
FRAMES = 128
EXPERTS = 32
CAP = 12
EP = 4
ROWS = EXPERTS * EP * CAP
EPSILON = 1e-06
BF16 = jnp.bfloat16
F32 = jnp.float32
NT = (((1,), (1,)), ((), ()))
TN = (((0,), (0,)), ((), ()))


def iota(shape, dim):
    return lax.broadcasted_iota(jnp.int32, shape, dim)


def ones_where(mask):
    return jnp.where(mask, 1.0, 0.0).astype(BF16)


def matmul(a, b, dims=(((1,), (0,)), ((), ()))):
    return lax.dot_general(a, b, dims, preferred_element_type=F32)


PACK = EXPERTS * 16
CHUNK = EXPERTS * CAP
GROUP = 16
EXTRA = 16


def column_block(j):
    return slice(256 * j, 256 * (j + 1))


def picked(ids, valid, places):
    ids = jnp.where(valid, ids, -1).astype(F32)
    return ones_where(jnp.logical_or(ids == places[0], ids == places[1]))


def dispatch_x_kernel(stream_ref, grad_ref, gain_ref, routes_ref, gates_ref, packed_ref, block_ref):
    s = stream_ref[...].astype(F32)
    inverse_rms = lax.rsqrt(jnp.mean(s * s, -1, keepdims=True) + EPSILON)
    normed = ((s * inverse_rms) * gain_ref[...]).astype(BF16)
    routes = routes_ref[...]
    expert = iota((EXPERTS, FRAMES), 0)
    named = [expert == routes[k : k + 1, :] for k in range(2)]
    count = ones_where(jnp.logical_or(named[0], named[1]))
    earlier = ones_where(iota((FRAMES, FRAMES), 0) < iota((FRAMES, FRAMES), 1))
    before = matmul(count, earlier)
    route = [routes[k : k + 1, :].astype(F32) for k in range(2)]
    slot = [jnp.sum(jnp.where(named[k], before, 0.0), 0, keepdims=True) for k in range(2)]
    places = [route[k] * CAP + slot[k] for k in range(2)]
    split = []
    for k in range(2):
        gate = gates_ref[k : k + 1, :]
        high = gate.astype(BF16).astype(F32)
        middle = (gate - high).astype(BF16).astype(F32)
        split += [high, middle, gate - high - middle]
    block_ref[0:FRAMES, :] = grad_ref[...]
    block_ref[FRAMES:, :] = jnp.zeros((EXTRA, D), BF16)
    extra = jnp.concatenate(route + slot + split + [jnp.zeros((EXTRA - 10, FRAMES), F32)], 0)
    block_ref[FRAMES:, 0:FRAMES] = extra.astype(BF16)
    row = iota((PACK, FRAMES), 0)
    lane = row & 15
    base = (row >> 4) * CAP
    main = picked(base + lane, lane < CAP, places)
    for j in range(3):
        last = picked(base + (lane - CAP) + 4 * j, lane >= CAP, places)
        c = column_block(j)
        packed_ref[:, c] = (matmul(main, normed[:, c]) + matmul(last, normed[:, 768:])).astype(BF16)


def dispatch_x(stream, grad, gain, routes, gates):
    return pl.pallas_call(
        dispatch_x_kernel,
        out_shape=(
            jax.ShapeDtypeStruct((PACK, 768), BF16),
            jax.ShapeDtypeStruct((FRAMES + EXTRA, D), BF16),
        ),
        name="dispatch_x",
    )(stream, grad, gain, routes, gates)


def dispatch_g_kernel(*refs):
    blocks, out_ref, pairs, keys = refs[:EP], refs[EP], refs[EP + 1], refs[EP + 2]
    step = pl.program_id(0)

    for q in range(EP):

        @pl.when(step == q)
        def _(q=q):
            extra = blocks[q][FRAMES:, 0:FRAMES].astype(F32)
            upright = extra.T
            g = blocks[q][0:FRAMES, :].astype(F32)
            for k in range(2):
                gate = upright[:, 4 + 3 * k : 5 + 3 * k] + upright[:, 5 + 3 * k : 6 + 3 * k]
                gate = gate + upright[:, 6 + 3 * k : 7 + 3 * k]
                pairs[k * FRAMES : (k + 1) * FRAMES, :] = (gate * g).astype(BF16)
                keys[k : k + 1, :] = extra[k : k + 1, :] * CAP + extra[2 + k : 3 + k, :]

    row = iota((PACK, FRAMES), 0)
    lane = row & 15
    base = (row >> 4) * CAP

    def pick(ids, valid):
        ids = jnp.where(valid, ids, -1).astype(F32)
        return jnp.concatenate([ones_where(ids == keys[k : k + 1, :]) for k in range(2)], 1)

    main = pick(base + lane, lane < CAP)
    for j in range(3):
        last = pick(base + (lane - CAP) + 4 * j, lane >= CAP)
        c = column_block(j)
        rows = matmul(main, pairs[:, c]) + matmul(last, pairs[:, 768:])
        out_ref[:, 0, :, c] = rows.astype(BF16).reshape(EXPERTS, 16, 256)


def dispatch_g(blocks):
    return pl.pallas_call(
        dispatch_g_kernel,
        grid=(EP,),
        in_specs=[pl.BlockSpec((FRAMES + EXTRA, D), lambda i: (0, 0))] * EP,
        out_specs=pl.BlockSpec((EXPERTS, 1, 16, 768), lambda i: (0, i, 0, 0)),
        out_shape=jax.ShapeDtypeStruct((EXPERTS, EP, 16, 768), BF16),
        scratch_shapes=[pltpu.VMEM((2 * FRAMES, D), BF16), pltpu.VMEM((8, FRAMES), F32)],
        name="dispatch_g",
    )(*blocks)


def fill_moves(moves, packed_dim):
    shape = (GROUP * 16, GROUP * CAP) if packed_dim == 0 else (GROUP * CAP, GROUP * 16)
    p = iota(shape, packed_dim)
    r = iota(shape, 1 - packed_dim)
    sender = (r * 1366) >> 14
    slot = r - sender * CAP
    same = (p >> 4) == sender
    lane = p & 15
    moves[0] = ones_where(jnp.logical_and(same, lane == slot))
    for j in range(3):
        hit = jnp.logical_and(same, lane == CAP + slot - 4 * j)
        moves[1 + j] = ones_where(jnp.logical_and(hit, (slot >> 2) == j))


def unpack(packed, moves, out_ref):
    for g in range(EXPERTS // GROUP):
        part = packed[GROUP * 16 * g : GROUP * 16 * (g + 1), :]
        rows = slice(GROUP * CAP * g, GROUP * CAP * (g + 1))
        out_ref[rows, 0:768] = matmul(moves[0], part).astype(BF16)
        last = matmul(moves[1], part[:, column_block(0)])
        last += matmul(moves[2], part[:, column_block(1)])
        last += matmul(moves[3], part[:, column_block(2)])
        out_ref[rows, 768:1024] = last.astype(BF16)


N_BLOCK = 256


def forward_kernel(count, *refs):
    parts, gate_ref, up_ref = refs[:count], refs[count], refs[count + 1]
    x_ref, a_ref, s_ref, acted_ref, moves = refs[-5:]

    @pl.when(pl.program_id(0) == 0)
    def _():
        fill_moves(moves, 1)
        unpack(jnp.concatenate([p[...] for p in parts], 0), moves, x_ref)

    x = x_ref[...]
    gate = matmul(x, gate_ref[...])
    up = matmul(x, up_ref[...])
    sig = jax.nn.sigmoid(gate)
    silu = gate * sig
    acted_ref[...] = (silu * up).astype(BF16)
    s_ref[...] = silu
    a_ref[...] = up * sig * (1.0 + gate * (1.0 - sig))


def expert_forward(q, parts, w_gate, w_up, filled):
    whole = [pl.BlockSpec(p.shape, lambda j: (0, 0)) for p in parts]
    weight = pl.BlockSpec((D, N_BLOCK), lambda j: (0, j))
    out = pl.BlockSpec((CHUNK, N_BLOCK), lambda j: (q, j))
    shape = lambda t: jax.ShapeDtypeStruct((ROWS, D), t)
    n = len(parts)
    return pl.pallas_call(
        lambda *refs: forward_kernel(n, *refs),
        grid=(D // N_BLOCK,),
        in_specs=whole + [weight] * 2 + [pl.BlockSpec(memory_space=pl.ANY)] * len(filled),
        out_specs=[pl.BlockSpec((CHUNK, D), lambda j: (q, 0)), out, out, out],
        out_shape=(shape(BF16), shape(F32), shape(F32), shape(BF16)),
        scratch_shapes=[pltpu.VMEM((4, GROUP * CAP, GROUP * 16), BF16)],
        input_output_aliases={n + 2 + i: i for i in range(len(filled))},
        name="expert_forward",
    )(*parts, w_gate, w_up, *filled)


def backward_kernel(
    order_ref, packed_ref, a_ref, s_ref, gate_ref, up_ref, down_ref, g_ref, dgate_ref, dup_ref, out_ref, moves, back
):
    @pl.when(pl.program_id(0) == 0)
    def _():
        fill_moves(moves, 1)
        fill_moves(back, 0)

    unpack(packed_ref[...].reshape(PACK, 768), moves, g_ref)
    dact = matmul(g_ref[...], down_ref[...], NT)
    dgate = (dact * a_ref[...]).astype(BF16)
    dup = (dact * s_ref[...]).astype(BF16)
    dgate_ref[...] = dgate
    dup_ref[...] = dup
    dx = (matmul(dgate, gate_ref[...], NT) + matmul(dup, up_ref[...], NT)).astype(BF16)
    for g in range(EXPERTS // GROUP):
        part = dx[GROUP * CAP * g : GROUP * CAP * (g + 1), :]
        for j in range(3):
            c = column_block(j)
            rows = matmul(back[0], part[:, c]) + matmul(back[1 + j], part[:, 768:])
            out_ref[GROUP * g : GROUP * (g + 1), 0, :, c] = rows.astype(BF16).reshape(GROUP, 16, 256)


def expert_backward(order, packed, a, s, w_gate, w_up, w_down):
    weight = pl.BlockSpec((D, D), lambda i, o: (0, 0), pipeline_mode=pl.Buffered(1))
    rows = pl.BlockSpec((CHUNK, D), lambda i, o: (i, 0))
    shape = jax.ShapeDtypeStruct((ROWS, D), BF16)
    return pl.pallas_call(
        backward_kernel,
        grid_spec=pltpu.PrefetchScalarGridSpec(
            num_scalar_prefetch=1,
            grid=(EP,),
            in_specs=[
                pl.BlockSpec((EXPERTS, 1, 16, 768), lambda i, o: (0, i, 0, 0)),
                rows,
                rows,
                weight,
                weight,
                weight,
            ],
            out_specs=[rows, rows, rows, pl.BlockSpec((EXPERTS, 1, 16, 768), lambda i, o: (0, o[i], 0, 0))],
            scratch_shapes=[
                pltpu.VMEM((4, GROUP * CAP, GROUP * 16), BF16),
                pltpu.VMEM((4, GROUP * 16, GROUP * CAP), BF16),
            ],
        ),
        out_shape=(shape, shape, shape, jax.ShapeDtypeStruct((EXPERTS, EP, 16, 768), BF16)),
        name="expert_backward",
    )(order, packed, a, s, w_gate, w_up, w_down)


WINDOW = LEFT + FRAMES
SCALE = 1.0 / math.sqrt(HEAD)
PAIRS = HEADS // 2


def one_head(pair, h):
    lane = iota(pair.shape, 1)
    mask = lane >= HEAD if h else lane < HEAD
    return jnp.where(mask, pair.astype(F32), 0.0).astype(BF16)


def probs_kernel(first_ref, q_ref, k2_ref, k1_ref, k0_ref, p_ref, stats_ref):
    keys = jnp.concatenate([k2_ref[...], k1_ref[...], k0_ref[...]], 0)
    q = q_ref[...]
    s = iota((WINDOW, FRAMES), 0)
    skipped = jnp.where(iota((WINDOW, FRAMES), 1) >= SPAN, SPAN, 0)
    allowed = jnp.logical_and(s >= skipped, s < skipped + (WINDOW - SPAN))
    allowed = jnp.logical_and(allowed, s >= first_ref[0])
    stats_ref[...] = jnp.zeros((2, 8, FRAMES), F32)
    for h in range(2):
        scores = matmul(keys, one_head(q, h), NT) * SCALE
        scores = jnp.where(allowed, scores, -jnp.inf)
        top = jnp.max(scores, 0, keepdims=True)
        e = jnp.exp(scores - top)
        inverse = 1.0 / jnp.sum(e, 0, keepdims=True)
        p_ref[h] = e * inverse
        stats_ref[h, 0:1, :] = top
        stats_ref[h, 1:2, :] = inverse


def attention_probs(first, q, k2, k1, k0):
    pair = pl.BlockSpec((FRAMES, 2 * HEAD), lambda i, *_: (0, i))
    heads = lambda n: pl.BlockSpec((2, n, FRAMES), lambda i, *_: (i, 0, 0))
    return pl.pallas_call(
        probs_kernel,
        grid_spec=pltpu.PrefetchScalarGridSpec(
            num_scalar_prefetch=1,
            grid=(PAIRS,),
            in_specs=[pair] * 4,
            out_specs=[heads(WINDOW), heads(8)],
        ),
        out_shape=(
            jax.ShapeDtypeStruct((HEADS, WINDOW, FRAMES), F32),
            jax.ShapeDtypeStruct((HEADS, 8, FRAMES), F32),
        ),
        name="attention_probs",
    )(first, q, k2, k1, k0)


def later_probs_kernel(q1_ref, q2_ref, stats1_ref, stats2_ref, k_ref, p_ref):
    k = k_ref[...]
    shape = (FRAMES, FRAMES)
    allowed = iota(shape, 0) >= jnp.where(iota(shape, 1) >= SPAN, SPAN, 0)
    for n, (q_ref, stats_ref) in enumerate(((q1_ref, stats1_ref), (q2_ref, stats2_ref))):
        q = q_ref[...]
        for h in range(2):
            scores = matmul(k, one_head(q, h), NT) * SCALE
            if n == 1:
                scores = jnp.where(allowed, scores, -jnp.inf)
            p_ref[h, n] = jnp.exp(scores - stats_ref[h, 0:1, :]) * stats_ref[h, 1:2, :]


def later_probs(q1, q2, stats1, stats2, k):
    pair = pl.BlockSpec((FRAMES, 2 * HEAD), lambda i: (0, i))
    stats = pl.BlockSpec((2, 8, FRAMES), lambda i: (i, 0, 0))
    return pl.pallas_call(
        later_probs_kernel,
        grid=(PAIRS,),
        in_specs=[pair, pair, stats, stats, pair],
        out_specs=pl.BlockSpec((2, 2, FRAMES, FRAMES), lambda i: (i, 0, 0, 0)),
        out_shape=jax.ShapeDtypeStruct((HEADS, 2, FRAMES, FRAMES), F32),
        name="later_probs",
    )(q1, q2, stats1, stats2, k)


def stream_grad_kernel(rows_ref, block_ref, stream_ref, gain_ref, o_ref, main, total):
    j = pl.program_id(0)
    upright = block_ref[FRAMES:, 0:FRAMES].astype(F32).T
    places = [upright[:, k : k + 1] * CAP + upright[:, 2 + k : 3 + k] for k in range(2)]
    row = iota((FRAMES, PACK * EP), 1)
    lane = row & 15
    base = (row >> 6) * CAP

    @pl.when(j == 0)
    def _():
        main[...] = picked(base + lane, lane < CAP, places)
        total[3] = jnp.zeros((FRAMES, 256), F32)

    rows = rows_ref[...]
    last = picked(base + (lane - CAP) + 4 * j, lane >= CAP, places)
    both = matmul(jnp.concatenate([main[...], last], 0), rows)
    total[j] = both[:FRAMES]
    total[3] += both[FRAMES:]

    @pl.when(j == 2)
    def _():
        dnormed = jnp.concatenate([total[c] for c in range(4)], 1)
        s = stream_ref[...].astype(F32)
        inverse_rms = lax.rsqrt(jnp.mean(s * s, -1, keepdims=True) + EPSILON)
        scaled = s * inverse_rms
        weighted = dnormed * gain_ref[...]
        mean = jnp.mean(weighted * scaled, -1, keepdims=True)
        grad = block_ref[0:FRAMES, :].astype(F32)
        o_ref[...] = (grad + inverse_rms * (weighted - scaled * mean)).astype(BF16)


def stream_gradient(returned, block, stream, gain):
    whole = lambda n: pl.BlockSpec((n, D), lambda j: (0, 0))
    return pl.pallas_call(
        stream_grad_kernel,
        grid=(3,),
        in_specs=[
            pl.BlockSpec((PACK * EP, 256), lambda j: (0, j)),
            whole(FRAMES + EXTRA),
            whole(FRAMES),
            whole(1),
        ],
        out_specs=whole(FRAMES),
        out_shape=jax.ShapeDtypeStruct((FRAMES, D), BF16),
        scratch_shapes=[pltpu.VMEM((FRAMES, PACK * EP), BF16), pltpu.VMEM((4, FRAMES, 256), F32)],
        name="stream_gradient",
    )(returned, block, stream, gain)


def own_grads_kernel(
    p_ref, o_ref, q_ref, k2_ref, k1_ref, k0_ref, v2_ref, v1_ref, v0_ref, dq_ref, dk_ref, dv_ref, delta_ref
):
    o, q = o_ref[...], q_ref[...]
    keys = jnp.concatenate([k2_ref[...], k1_ref[...], k0_ref[...]], 0)
    values = jnp.concatenate([v2_ref[...], v1_ref[...], v0_ref[...]], 0)
    delta_ref[...] = jnp.zeros((2, 8, FRAMES), F32)
    dq = dk = dv = 0.0
    for h in range(2):
        o_h, q_h, k_h = one_head(o, h), one_head(q, h), one_head(keys, h)
        probs = p_ref[h]
        rounded = probs.astype(BF16)
        dprob = matmul(values, o_h, NT)
        delta = jnp.sum(rounded.astype(F32) * dprob, 0, keepdims=True)
        delta_ref[h, 0:1, :] = delta
        dscore = (probs * (dprob - delta)).astype(BF16)
        dq += matmul(dscore, k_h, TN)
        dk += matmul(dscore[LEFT:], q_h)
        dv += matmul(rounded[LEFT:], o_h)
    dq_ref[...] = (dq * SCALE).astype(BF16)
    dk_ref[...] = dk
    dv_ref[...] = dv


def own_grads(probs, o, q, ks, vs):
    pair = pl.BlockSpec((FRAMES, 2 * HEAD), lambda i: (0, i))
    heads = lambda n: pl.BlockSpec((2, n, FRAMES), lambda i: (i, 0, 0))
    out = lambda t: jax.ShapeDtypeStruct((FRAMES, D), t)
    return pl.pallas_call(
        own_grads_kernel,
        grid=(PAIRS,),
        in_specs=[heads(WINDOW)] + [pair] * 8,
        out_specs=[pair, pair, pair, heads(8)],
        out_shape=(out(BF16), out(F32), out(F32), jax.ShapeDtypeStruct((HEADS, 8, FRAMES), F32)),
        name="own_grads",
    )(probs, o, q, *ks, *vs)


def later_grads_kernel(
    p_ref, o1_ref, o2_ref, q1_ref, q2_ref, delta1_ref, delta2_ref, v_ref, dk_ref, dv_ref, keys_ref, values_ref
):
    v = v_ref[...]
    dk, dv = dk_ref[...], dv_ref[...]
    sources = ((o1_ref, q1_ref, delta1_ref), (o2_ref, q2_ref, delta2_ref))
    for n, (o_ref, q_ref, delta_ref) in enumerate(sources):
        o, q = o_ref[...], q_ref[...]
        for h in range(2):
            o_h, q_h = one_head(o, h), one_head(q, h)
            probs = p_ref[h, n]
            dprob = matmul(v, o_h, NT)
            dscore = (probs * (dprob - delta_ref[h, 0:1, :])).astype(BF16)
            dk += matmul(dscore, q_h)
            dv += matmul(probs.astype(BF16), o_h)
    keys_ref[...] = (dk * SCALE).astype(BF16)
    values_ref[...] = dv.astype(BF16)


def later_grads(probs, os, qs, deltas, v, dk, dv):
    pair = pl.BlockSpec((FRAMES, 2 * HEAD), lambda i: (0, i))
    stats = pl.BlockSpec((2, 8, FRAMES), lambda i: (i, 0, 0))
    return pl.pallas_call(
        later_grads_kernel,
        grid=(PAIRS,),
        in_specs=[pl.BlockSpec((2, 2, FRAMES, FRAMES), lambda i: (i, 0, 0, 0))]
        + [pair] * 4
        + [stats] * 2
        + [pair] * 3,
        out_specs=[pair, pair],
        out_shape=(jax.ShapeDtypeStruct((FRAMES, D), BF16),) * 2,
        name="later_grads",
    )(probs, *os, *qs, *deltas, v, dk, dv)


def turned(x, distance):
    return lax.ppermute(x, "ep", [(i, (i + distance) % EP) for i in range(EP)])


def shifted(x, distance):
    count = lax.axis_size("tm") * lax.axis_size("ep")
    route = [(i, i + distance) for i in range(count) if 0 <= i + distance < count]
    return lax.ppermute(x, ("tm", "ep"), route)


def exchanged(x, axes):
    return lax.all_to_all(x, axes, split_axis=0, concat_axis=0, tiled=True)


def body(
    queries, keys, values, stream, grad_out, norm_gain, gate_probs, routes, w_gate, w_up, w_down
):
    gain = norm_gain.reshape(1, D)
    weight_gate, weight_up, weight_down = w_gate[0], w_up[0], w_down[0]
    row, column = lax.axis_index("tm"), lax.axis_index("ep")
    order = jnp.stack([column, (column + 3) % EP, (column + 1) % EP, (column + 2) % EP]).astype(jnp.int32)
    packed, block = dispatch_x(stream, grad_out, gain, routes.T, gate_probs.T)
    own = exchanged(packed.reshape(EXPERTS, 16, 768), "tm").reshape(PACK, 768)
    blocks = (block, turned(block, 1), turned(block, -1), turned(block, 2))
    left, right = turned(own, 1), turned(own, -1)
    half = PACK // 2
    top, bottom = turned(left[:half], 1), turned(right[half:], -1)
    sent_g = dispatch_g(blocks).reshape(EXPERTS, EP * 16, 768)
    packed_g = exchanged(sent_g, "tm").reshape(EXPERTS, EP, 16, 768)
    filled = ()
    for q, parts in enumerate(((own,), (left,), (right,), (top, bottom))):
        filled = expert_forward(q, parts, weight_gate, weight_up, filled)
    x_rows, a, s, acted = filled
    g_rows, dgate, dup, dx = expert_backward(order, packed_g, a, s, weight_gate, weight_up, weight_down)
    returned = exchanged(dx.reshape(EXPERTS * EP, 16, 768), ("tm", "ep")).reshape(PACK * EP, 768)
    gate_grad = jnp.dot(x_rows.T, dgate, preferred_element_type=F32)
    up_grad = jnp.dot(x_rows.T, dup, preferred_element_type=F32)
    down_grad = jnp.dot(acted.T, g_rows, preferred_element_type=F32)
    ks = (shifted(keys, 2), shifted(keys, 1), keys)
    vs = (shifted(values, 2), shifted(values, 1), values)
    qs = (shifted(queries, -1), shifted(queries, -2))
    position = row * lax.axis_size("ep") + column
    first = jnp.maximum(LEFT - position * FRAMES, 0).astype(jnp.int32).reshape(1)
    probs, stats = attention_probs(first, queries, *ks)
    later = later_probs(*qs, shifted(stats, -1), shifted(stats, -2), keys)
    stream_grad = stream_gradient(returned, block, stream, gain)
    later_o = (shifted(stream_grad, -1), shifted(stream_grad, -2))
    grad_q, own_k, own_v, delta = own_grads(probs, stream_grad, queries, ks, vs)
    deltas = (shifted(delta, -1), shifted(delta, -2))
    grad_k, grad_v = later_grads(later, later_o, qs, deltas, values, own_k, own_v)
    return (
        grad_q,
        grad_k,
        grad_v,
        stream_grad,
        gate_grad[None],
        up_grad[None],
        down_grad[None],
    )


def solution(mesh):
    frames = P(("tm", "ep"), None)
    columns, rows = P("tm", None, "ep"), P("tm", "ep", None)
    return jax.shard_map(
        body,
        mesh=mesh,
        in_specs=(frames,) * 5 + (P(), frames, frames, columns, columns, rows),
        out_specs=(frames,) * 4 + (columns, columns, rows),
        check_vma=False,
    )
```

```python
import math

import jax
import jax.numpy as jnp
from jax import lax
from jax.experimental import pallas as pl
from jax.experimental.pallas import tpu as pltpu
from jax.sharding import PartitionSpec as P


D = 1024
HEADS = 16
HEAD = 64
SPAN = 64
LEFT = 256
FRAMES = 128
EXPERTS = 32
CAP = 12
EP = 4
ROWS = EXPERTS * EP * CAP
EPSILON = 1e-06
BF16 = jnp.bfloat16
F32 = jnp.float32
NT = (((1,), (1,)), ((), ()))
TN = (((0,), (0,)), ((), ()))


def iota(shape, dim):
    return lax.broadcasted_iota(jnp.int32, shape, dim)


def ones_where(mask):
    return jnp.where(mask, 1.0, 0.0).astype(BF16)


def matmul(a, b, dims=(((1,), (0,)), ((), ()))):
    return lax.dot_general(a, b, dims, preferred_element_type=F32)


PACK = EXPERTS * 8
WIDE = 1536
CHUNK = EXPERTS * CAP
HALF = D // 2
EXTRA = 16


def picked(ids, valid, places):
    ids = jnp.where(valid, ids, -1).astype(F32)
    return ones_where(jnp.logical_or(ids == places[0], ids == places[1]))


def dispatch_x_kernel(
    stream_ref, grad_ref, gain_ref, routes_ref, gates_ref, k_ref, v_ref, packed_ref, block_ref, both_ref
):
    s = stream_ref[...].astype(F32)
    inverse_rms = lax.rsqrt(jnp.mean(s * s, -1, keepdims=True) + EPSILON)
    normed = ((s * inverse_rms) * gain_ref[...]).astype(BF16)
    routes = routes_ref[...]
    expert = iota((EXPERTS, FRAMES), 0)
    named = [expert == routes[k : k + 1, :] for k in range(2)]
    count = ones_where(jnp.logical_or(named[0], named[1]))
    earlier = ones_where(iota((FRAMES, FRAMES), 0) < iota((FRAMES, FRAMES), 1))
    before = matmul(count, earlier)
    route = [routes[k : k + 1, :].astype(F32) for k in range(2)]
    slot = [jnp.sum(jnp.where(named[k], before, 0.0), 0, keepdims=True) for k in range(2)]
    places = [route[k] * CAP + slot[k] for k in range(2)]
    split = []
    for k in range(2):
        gate = gates_ref[k : k + 1, :]
        high = gate.astype(BF16).astype(F32)
        middle = (gate - high).astype(BF16).astype(F32)
        split += [high, middle, gate - high - middle]
    block_ref[0:FRAMES, :] = grad_ref[...]
    block_ref[FRAMES:, :] = jnp.zeros((EXTRA, D), BF16)
    extra = jnp.concatenate(route + slot + split + [jnp.zeros((EXTRA - 10, FRAMES), F32)], 0)
    block_ref[FRAMES:, 0:FRAMES] = extra.astype(BF16)
    both_ref[0] = k_ref[...]
    both_ref[1] = v_ref[...]
    row = iota((PACK, FRAMES), 0)
    r = row & 7
    base = (row >> 3) * CAP
    main = picked(base + r, r < 8, places)
    low = picked(base + 8 + r, r < 4, places)
    high = picked(base + 4 + r, r >= 4, places)
    packed_ref[:, 0:D] = matmul(main, normed).astype(BF16)
    packed_ref[:, D:] = (matmul(low, normed[:, :HALF]) + matmul(high, normed[:, HALF:])).astype(BF16)


def dispatch_x(stream, grad, gain, routes, gates, keys, values):
    return pl.pallas_call(
        dispatch_x_kernel,
        out_shape=(
            jax.ShapeDtypeStruct((PACK, WIDE), BF16),
            jax.ShapeDtypeStruct((FRAMES + EXTRA, D), BF16),
            jax.ShapeDtypeStruct((2, FRAMES, D), BF16),
        ),
        name="dispatch_x",
    )(stream, grad, gain, routes, gates, keys, values)


def dispatch_g_kernel(*refs):
    blocks, out_ref, pairs, keys = refs[:EP], refs[EP], refs[EP + 1], refs[EP + 2]
    step = pl.program_id(0)

    for q in range(EP):

        @pl.when(step == q)
        def _(q=q):
            extra = blocks[q][FRAMES:, 0:FRAMES].astype(F32)
            upright = extra.T
            g = blocks[q][0:FRAMES, :].astype(F32)
            for k in range(2):
                gate = upright[:, 4 + 3 * k : 5 + 3 * k] + upright[:, 5 + 3 * k : 6 + 3 * k]
                gate = gate + upright[:, 6 + 3 * k : 7 + 3 * k]
                pairs[k * FRAMES : (k + 1) * FRAMES, :] = (gate * g).astype(BF16)
                keys[k : k + 1, :] = extra[k : k + 1, :] * CAP + extra[2 + k : 3 + k, :]

    row = iota((PACK, FRAMES), 0)
    r = row & 7
    base = (row >> 3) * CAP

    def pick(ids, valid):
        ids = jnp.where(valid, ids, -1).astype(F32)
        return jnp.concatenate([ones_where(ids == keys[k : k + 1, :]) for k in range(2)], 1)

    main = pick(base + r, r < 8)
    low = pick(base + 8 + r, r < 4)
    high = pick(base + 4 + r, r >= 4)
    out_ref[:, 0, :, 0:D] = matmul(main, pairs[...]).reshape(EXPERTS, 8, D).astype(BF16)
    rest = matmul(low, pairs[:, :HALF]) + matmul(high, pairs[:, HALF:])
    out_ref[:, 0, :, D:] = rest.reshape(EXPERTS, 8, HALF).astype(BF16)


def dispatch_g(blocks):
    return pl.pallas_call(
        dispatch_g_kernel,
        grid=(EP,),
        in_specs=[pl.BlockSpec((FRAMES + EXTRA, D), lambda i: (0, 0))] * EP,
        out_specs=pl.BlockSpec((EXPERTS, 1, 8, WIDE), lambda i: (0, i, 0, 0)),
        out_shape=jax.ShapeDtypeStruct((EXPERTS, EP, 8, WIDE), BF16),
        scratch_shapes=[pltpu.VMEM((2 * FRAMES, D), BF16), pltpu.VMEM((8, FRAMES), F32)],
        name="dispatch_g",
    )(*blocks)


def fill_moves(moves, packed_dim):
    shape = (PACK, PACK // 2) if packed_dim == 0 else (PACK // 2, PACK)
    p = iota(shape, packed_dim)
    r = iota(shape, 1 - packed_dim)
    same = (p >> 3) == (r >> 2)
    for n in range(2):
        moves[n] = ones_where(jnp.logical_and(same, (p & 7) == (r & 3) + 4 * n))


def unpack(packed, moves, out_ref, start):
    out_ref[start : start + PACK, :] = packed[:, 0:D]
    for n in range(2):
        rest = matmul(moves[n], packed[:, D:]).astype(BF16)
        out_ref[start + PACK : start + CHUNK, n * HALF : (n + 1) * HALF] = rest


N_BLOCK = 256


def forward_kernel(count, *refs):
    parts, gate_ref, up_ref = refs[:count], refs[count], refs[count + 1]
    x_ref, a_ref, s_ref, acted_ref, moves = refs[-5:]

    @pl.when(pl.program_id(0) == 0)
    def _():
        fill_moves(moves, 1)
        for n, part in enumerate(parts):
            unpack(part[...], moves, x_ref, n * CHUNK)

    x = x_ref[...]
    gate = matmul(x, gate_ref[...])
    up = matmul(x, up_ref[...])
    sig = jax.nn.sigmoid(gate)
    silu = gate * sig
    acted_ref[...] = (silu * up).astype(BF16)
    s_ref[...] = silu
    a_ref[...] = up * sig * (1.0 + gate * (1.0 - sig))


def expert_forward(q, parts, w_gate, w_up, filled):
    rows = len(parts) * CHUNK
    whole = [pl.BlockSpec(p.shape, lambda j: (0, 0)) for p in parts]
    weight = pl.BlockSpec((D, N_BLOCK), lambda j: (0, j))
    out = pl.BlockSpec((rows, N_BLOCK), lambda j: (q, j))
    shape = lambda t: jax.ShapeDtypeStruct((ROWS, D), t)
    n = len(parts)
    return pl.pallas_call(
        lambda *refs: forward_kernel(n, *refs),
        grid=(D // N_BLOCK,),
        in_specs=whole + [weight] * 2 + [pl.BlockSpec(memory_space=pl.ANY)] * len(filled),
        out_specs=[pl.BlockSpec((rows, D), lambda j: (q, 0)), out, out, out],
        out_shape=(shape(BF16), shape(F32), shape(F32), shape(BF16)),
        scratch_shapes=[pltpu.VMEM((2, PACK // 2, PACK), BF16)],
        input_output_aliases={n + 2 + i: i for i in range(len(filled))},
        name="expert_forward",
    )(*parts, w_gate, w_up, *filled)


def backward_kernel(
    column_ref, packed_ref, a_ref, s_ref, gate_ref, up_ref, down_ref, g_ref, dgate_ref, dup_ref, out_ref, moves, back
):
    @pl.when(pl.program_id(0) == 0)
    def _():
        fill_moves(moves, 1)
        fill_moves(back, 0)

    unpack(packed_ref[...].astype(F32).reshape(PACK, WIDE).astype(BF16), moves, g_ref, 0)
    dact = matmul(g_ref[...], down_ref[...], NT)
    dgate = (dact * a_ref[...]).astype(BF16)
    dup = (dact * s_ref[...]).astype(BF16)
    dgate_ref[...] = dgate
    dup_ref[...] = dup
    dx = matmul(dgate, gate_ref[...], NT) + matmul(dup, up_ref[...], NT)
    out_ref[:, 0, :, 0:D] = dx[:PACK].reshape(EXPERTS, 8, D).astype(BF16)
    last = dx[PACK:].astype(BF16)
    rest = matmul(back[0], last[:, :HALF]) + matmul(back[1], last[:, HALF:])
    out_ref[:, 0, :, D:] = rest.reshape(EXPERTS, 8, HALF).astype(BF16)


def expert_backward(column, packed, a, s, w_gate, w_up, w_down):
    def home(q, c):
        return (c[0] + jnp.where(q < 2, 3 - 2 * q, 2 * q - 4)) & 3

    weight = pl.BlockSpec((D, D), lambda i, c: (0, 0), pipeline_mode=pl.Buffered(1))
    rows = pl.BlockSpec((CHUNK, D), lambda i, c: (i, 0))
    shape = jax.ShapeDtypeStruct((ROWS, D), BF16)
    return pl.pallas_call(
        backward_kernel,
        grid_spec=pltpu.PrefetchScalarGridSpec(
            num_scalar_prefetch=1,
            grid=(EP,),
            in_specs=[
                pl.BlockSpec((EXPERTS, 1, 8, WIDE), lambda i, c: (0, i, 0, 0)),
                rows,
                rows,
                weight,
                weight,
                weight,
            ],
            out_specs=[rows, rows, rows, pl.BlockSpec((EXPERTS, 1, 8, WIDE), lambda i, c: (0, home(i, c), 0, 0))],
            scratch_shapes=[
                pltpu.VMEM((2, PACK // 2, PACK), BF16),
                pltpu.VMEM((2, PACK, PACK // 2), BF16),
            ],
        ),
        out_shape=(shape, shape, shape, jax.ShapeDtypeStruct((EXPERTS, EP, 8, WIDE), BF16)),
        name="expert_backward",
    )(column, packed, a, s, w_gate, w_up, w_down)


WINDOW = LEFT + FRAMES
SCALE = 1.0 / math.sqrt(HEAD)
PAIR = 2 * HEAD
STEP_PAIRS = 2
WIDTH = STEP_PAIRS * PAIR
STEP_HEADS = 2 * STEP_PAIRS
STEPS = HEADS // STEP_HEADS


def one_head(pair, h):
    lane = iota(pair.shape, 1)
    mask = lane >= HEAD if h else lane < HEAD
    return jnp.where(mask, pair.astype(F32), 0.0).astype(BF16)


def lanes(n):
    return slice(n * PAIR, (n + 1) * PAIR)


def columns_spec(*lead):
    return pl.BlockSpec((*lead, WIDTH), lambda i, *_: (0,) * len(lead) + (i,))


def heads_spec(*rest):
    return pl.BlockSpec((STEP_HEADS, *rest), lambda i, *_: (i,) + (0,) * len(rest))


def probs_kernel(first_ref, q_ref, both2_ref, both1_ref, k_ref, v_ref, p_ref, stats_ref, attn_ref):
    s = iota((WINDOW, FRAMES), 0)
    skipped = jnp.where(iota((WINDOW, FRAMES), 1) >= SPAN, SPAN, 0)
    allowed = jnp.logical_and(s >= skipped, s < skipped + (WINDOW - SPAN))
    allowed = jnp.logical_and(allowed, s >= first_ref[0])
    stats_ref[...] = jnp.zeros((STEP_HEADS, 8, FRAMES), F32)
    for n in range(STEP_PAIRS):
        c = lanes(n)
        keys = jnp.concatenate([both2_ref[0, :, c], both1_ref[0, :, c], k_ref[:, c]], 0)
        values = jnp.concatenate([both2_ref[1, :, c], both1_ref[1, :, c], v_ref[:, c]], 0)
        q = q_ref[:, c]
        attn = 0.0
        for h in range(2):
            at = 2 * n + h
            scores = matmul(keys, one_head(q, h), NT) * SCALE
            scores = jnp.where(allowed, scores, -jnp.inf)
            top = jnp.max(scores, 0, keepdims=True)
            e = jnp.exp(scores - top)
            inverse = 1.0 / jnp.sum(e, 0, keepdims=True)
            probs = e * inverse
            p_ref[at] = probs
            attn += matmul(probs.astype(BF16), one_head(values, h), TN)
            stats_ref[at, 0:1, :] = top
            stats_ref[at, 1:2, :] = inverse
        attn_ref[:, c] = attn


def attention_probs(first, q, both2, both1, k, v):
    both, one = columns_spec(2, FRAMES), columns_spec(FRAMES)
    return pl.pallas_call(
        probs_kernel,
        grid_spec=pltpu.PrefetchScalarGridSpec(
            num_scalar_prefetch=1,
            grid=(STEPS,),
            in_specs=[one, both, both, one, one],
            out_specs=[heads_spec(WINDOW, FRAMES), heads_spec(8, FRAMES), one],
        ),
        out_shape=(
            jax.ShapeDtypeStruct((HEADS, WINDOW, FRAMES), F32),
            jax.ShapeDtypeStruct((HEADS, 8, FRAMES), F32),
            jax.ShapeDtypeStruct((FRAMES, D), F32),
        ),
        name="attention_probs",
    )(first, q, both2, both1, k, v)


def later_probs_kernel(q1_ref, q2_ref, stats1_ref, stats2_ref, k_ref, p_ref):
    shape = (FRAMES, FRAMES)
    allowed = iota(shape, 0) >= jnp.where(iota(shape, 1) >= SPAN, SPAN, 0)
    for n in range(STEP_PAIRS):
        k = k_ref[:, lanes(n)]
        for m, (q_ref, stats_ref) in enumerate(((q1_ref, stats1_ref), (q2_ref, stats2_ref))):
            q = q_ref[:, lanes(n)]
            for h in range(2):
                at = 2 * n + h
                scores = matmul(k, one_head(q, h), NT) * SCALE
                if m == 1:
                    scores = jnp.where(allowed, scores, -jnp.inf)
                p_ref[at, m] = jnp.exp(scores - stats_ref[at, 0:1, :]) * stats_ref[at, 1:2, :]


def later_probs(q1, q2, stats1, stats2, k):
    one, stats = columns_spec(FRAMES), heads_spec(8, FRAMES)
    return pl.pallas_call(
        later_probs_kernel,
        grid=(STEPS,),
        in_specs=[one, one, stats, stats, one],
        out_specs=heads_spec(2, FRAMES, FRAMES),
        out_shape=jax.ShapeDtypeStruct((HEADS, 2, FRAMES, FRAMES), F32),
        name="later_probs",
    )(q1, q2, stats1, stats2, k)


def thirds(x):
    high = x.astype(BF16)
    rest = x - high.astype(F32)
    middle = rest.astype(BF16)
    return high, middle, (rest - middle.astype(F32)).astype(BF16)


def stream_grad_kernel(rows_ref, block_ref, stream_ref, gain_ref, attn_ref, o_ref, sent_ref, main, total):
    j = pl.program_id(0)
    upright = block_ref[FRAMES:, 0:FRAMES].astype(F32).T
    places = [upright[:, k : k + 1] * CAP + upright[:, 2 + k : 3 + k] for k in range(2)]
    row = iota((FRAMES, PACK * EP), 1)
    r = row & 7
    base = (row >> 5) * CAP

    @pl.when(j == 0)
    def _():
        main[...] = picked(base + r, r < 8, places)

    @pl.when(j < 2)
    def _():
        total[j] = matmul(main[...], rows_ref[...])

    @pl.when(j == 2)
    def _():
        low = picked(base + 8 + r, r < 4, places)
        high = picked(base + 4 + r, r >= 4, places)
        rest = matmul(jnp.concatenate([low, high], 0), rows_ref[...])
        dnormed = jnp.concatenate([total[0] + rest[:FRAMES], total[1] + rest[FRAMES:]], 1)
        s = stream_ref[...].astype(F32)
        inverse_rms = lax.rsqrt(jnp.mean(s * s, -1, keepdims=True) + EPSILON)
        scaled = s * inverse_rms
        weighted = dnormed * gain_ref[...]
        mean = jnp.mean(weighted * scaled, -1, keepdims=True)
        grad = block_ref[0:FRAMES, :].astype(F32)
        o = (grad + inverse_rms * (weighted - scaled * mean)).astype(BF16)
        o_ref[...] = o
        sent_ref[0:FRAMES, :] = o
        head = ones_where((iota((HEADS, D), 1) >> 6) == iota((HEADS, D), 0))
        delta = 0.0
        for part in thirds(o.astype(F32) * attn_ref[...]):
            delta += matmul(head, part, NT)
        sent_ref[FRAMES:, :] = jnp.concatenate(
            [*thirds(delta), jnp.zeros((HEADS, D - 3 * FRAMES), BF16)], 1
        )


def stream_gradient(returned, block, stream, gain, attn):
    whole = lambda n: pl.BlockSpec((n, D), lambda j: (0, 0))
    return pl.pallas_call(
        stream_grad_kernel,
        grid=(3,),
        in_specs=[
            pl.BlockSpec((PACK * EP, HALF), lambda j: (0, j)),
            whole(FRAMES + EXTRA),
            whole(FRAMES),
            whole(1),
            whole(FRAMES),
        ],
        out_specs=[whole(FRAMES), whole(FRAMES + HEADS)],
        out_shape=(
            jax.ShapeDtypeStruct((FRAMES, D), BF16),
            jax.ShapeDtypeStruct((FRAMES + HEADS, D), BF16),
        ),
        scratch_shapes=[pltpu.VMEM((FRAMES, PACK * EP), BF16), pltpu.VMEM((2, FRAMES, HALF), F32)],
        name="stream_gradient",
    )(returned, block, stream, gain, attn)


DELTA_SPEC = pl.BlockSpec((HEADS, 3 * FRAMES), lambda i: (FRAMES // HEADS, 0))


def delta_of(ref):
    part = lambda n: ref[:, n * FRAMES : (n + 1) * FRAMES].astype(F32)
    return part(0) + part(1) + part(2)


def own_grads_kernel(
    p_ref, o_ref, extra_ref, q_ref, both2_ref, both1_ref, k_ref, v_ref, dq_ref, dk_ref, dv_ref, deltas
):
    deltas[...] = delta_of(extra_ref)
    for n in range(STEP_PAIRS):
        c = lanes(n)
        o, q = o_ref[:, c], q_ref[:, c]
        keys = jnp.concatenate([both2_ref[0, :, c], both1_ref[0, :, c], k_ref[:, c]], 0)
        values = jnp.concatenate([both2_ref[1, :, c], both1_ref[1, :, c], v_ref[:, c]], 0)
        dq = dk = dv = 0.0
        for h in range(2):
            at = 2 * n + h
            o_h, q_h, k_h = one_head(o, h), one_head(q, h), one_head(keys, h)
            probs = p_ref[at]
            delta = deltas[pl.ds(STEP_HEADS * pl.program_id(0) + at, 1), :]
            dscore = (probs * (matmul(values, o_h, NT) - delta)).astype(BF16)
            dq += matmul(dscore, k_h, TN)
            dk += matmul(dscore[LEFT:], q_h)
            dv += matmul(probs[LEFT:].astype(BF16), o_h)
        dq_ref[:, c] = (dq * SCALE).astype(BF16)
        dk_ref[:, c] = dk
        dv_ref[:, c] = dv


def own_grads(probs, sent, q, both2, both1, keys, values):
    one, both = columns_spec(FRAMES), columns_spec(2, FRAMES)
    out = lambda t: jax.ShapeDtypeStruct((FRAMES, D), t)
    return pl.pallas_call(
        own_grads_kernel,
        grid=(STEPS,),
        in_specs=[heads_spec(WINDOW, FRAMES), one, DELTA_SPEC, one, both, both, one, one],
        out_specs=[one, one, one],
        out_shape=(out(BF16), out(F32), out(F32)),
        scratch_shapes=[pltpu.VMEM((HEADS, FRAMES), F32)],
        name="own_grads",
    )(probs, sent, sent, q, both2, both1, keys, values)


def later_grads_kernel(
    p_ref, o1_ref, o2_ref, extra1_ref, extra2_ref, q1_ref, q2_ref, v_ref, dk_ref, dv_ref, keys_ref, values_ref, deltas
):
    deltas[0] = delta_of(extra1_ref)
    deltas[1] = delta_of(extra2_ref)
    for n in range(STEP_PAIRS):
        c = lanes(n)
        v = v_ref[:, c]
        dk, dv = dk_ref[:, c], dv_ref[:, c]
        for m, (o_ref, q_ref) in enumerate(((o1_ref, q1_ref), (o2_ref, q2_ref))):
            o, q = o_ref[:, c], q_ref[:, c]
            for h in range(2):
                at = 2 * n + h
                o_h, q_h = one_head(o, h), one_head(q, h)
                probs = p_ref[at, m]
                delta = deltas[m, pl.ds(STEP_HEADS * pl.program_id(0) + at, 1), :]
                dscore = (probs * (matmul(v, o_h, NT) - delta)).astype(BF16)
                dk += matmul(dscore, q_h)
                dv += matmul(probs.astype(BF16), o_h)
        keys_ref[:, c] = (dk * SCALE).astype(BF16)
        values_ref[:, c] = dv.astype(BF16)


def later_grads(probs, os, qs, v, dk, dv):
    one = columns_spec(FRAMES)
    return pl.pallas_call(
        later_grads_kernel,
        grid=(STEPS,),
        in_specs=[heads_spec(2, FRAMES, FRAMES), one, one, DELTA_SPEC, DELTA_SPEC] + [one] * 5,
        out_specs=[one, one],
        out_shape=(jax.ShapeDtypeStruct((FRAMES, D), BF16),) * 2,
        scratch_shapes=[pltpu.VMEM((2, HEADS, FRAMES), F32)],
        name="later_grads",
    )(probs, *os, *os, *qs, v, dk, dv)


def turned(x, distance):
    return lax.ppermute(x, "ep", [(i, (i + distance) % EP) for i in range(EP)])


def shifted(x, distance):
    count = lax.axis_size("tm") * lax.axis_size("ep")
    route = [(i, i + distance) for i in range(count) if 0 <= i + distance < count]
    return lax.ppermute(x, ("tm", "ep"), route)


def exchanged(x, axes):
    return lax.all_to_all(x, axes, split_axis=0, concat_axis=0, tiled=True)


def step(
    queries, keys, values, stream, grad_out, norm_gain, gate_probs, routes, w_gate, w_up, w_down
):
    gain = norm_gain.reshape(1, D)
    weight_gate, weight_up, weight_down = w_gate[0], w_up[0], w_down[0]
    row, column = lax.axis_index("tm"), lax.axis_index("ep")
    packed, block, both = dispatch_x(
        stream, grad_out, gain, routes.T, gate_probs.T, keys, values
    )
    block_left = turned(block, 1)
    block_right = turned(block, -1)
    block_far = turned(block, 2)
    own = exchanged(packed.reshape(EXPERTS, 8, WIDE), "tm").reshape(PACK, WIDE)
    left = turned(own, 1)
    right = turned(own, -1)
    far = turned(left, 1)
    sent_g = dispatch_g((block_left, block_right, block, block_far)).reshape(EXPERTS, EP * 8, WIDE)
    packed_g = exchanged(sent_g, "tm").reshape(EXPERTS, EP, 8, WIDE)
    filled = expert_forward(2, (own,), weight_gate, weight_up, ())
    filled = expert_forward(0, (left, right), weight_gate, weight_up, filled)
    x_rows, a, s, acted = expert_forward(3, (far,), weight_gate, weight_up, filled)
    both1 = shifted(both, 1)
    both2 = shifted(both, 2)
    q1 = shifted(queries, -1)
    q2 = shifted(queries, -2)
    g_rows, dgate, dup, dx = expert_backward(
        column.astype(jnp.int32).reshape(1), packed_g, a, s, weight_gate, weight_up, weight_down
    )
    returned = exchanged(dx.reshape(EXPERTS * EP, 8, WIDE), ("tm", "ep")).reshape(PACK * EP, WIDE)
    gate_grad = jnp.dot(x_rows.T, dgate, preferred_element_type=F32)
    up_grad = jnp.dot(x_rows.T, dup, preferred_element_type=F32)
    down_grad = jnp.dot(acted.T, g_rows, preferred_element_type=F32)
    position = row * lax.axis_size("ep") + column
    first = jnp.maximum(LEFT - position * FRAMES, 0).astype(jnp.int32).reshape(1)
    probs, stats, attn = attention_probs(first, queries, both2, both1, keys, values)
    stats1 = shifted(stats, -1)
    stats2 = shifted(stats, -2)
    later = later_probs(q1, q2, stats1, stats2, keys)
    returned, later, probs, gate_grad, up_grad, down_grad = lax.optimization_barrier(
        (returned, later, probs, gate_grad, up_grad, down_grad)
    )
    stream_grad, sent_o = stream_gradient(returned, block, stream, gain, attn)
    o1 = shifted(sent_o, -1)
    o2 = shifted(sent_o, -2)
    grad_q, own_k, own_v = own_grads(probs, sent_o, queries, both2, both1, keys, values)
    grad_k, grad_v = later_grads(later, (o1, o2), (q1, q2), values, own_k, own_v)
    return (
        grad_q,
        grad_k,
        grad_v,
        stream_grad,
        gate_grad[None],
        up_grad[None],
        down_grad[None],
    )


def solution(mesh):
    frames = P(("tm", "ep"), None)
    columns, rows = P("tm", None, "ep"), P("tm", "ep", None)
    return jax.shard_map(
        step,
        mesh=mesh,
        in_specs=(frames,) * 5 + (P(), frames, frames, columns, columns, rows),
        out_specs=(frames,) * 4 + (columns, columns, rows),
        check_vma=False,
    )
```

```python
import math

import jax
import jax.numpy as jnp
from jax import lax
from jax.experimental import pallas as pl
from jax.experimental.pallas import tpu as pltpu
from jax.sharding import PartitionSpec as P


D = 1024
HEADS = 16
HEAD = 64
SPAN = 64
LEFT = 256
FRAMES = 128
EXPERTS = 32
CAP = 12
EP = 4
ROWS = EXPERTS * EP * CAP
EPSILON = 1e-06
BF16 = jnp.bfloat16
F32 = jnp.float32
NT = (((1,), (1,)), ((), ()))
TN = (((0,), (0,)), ((), ()))


VMEM_SPEC = pl.BlockSpec(memory_space=pltpu.VMEM)


def iota(shape, dim):
    return lax.broadcasted_iota(jnp.int32, shape, dim)


def ones_where(mask):
    return jnp.where(mask, 1.0, 0.0).astype(BF16)


def matmul(a, b, dims=(((1,), (0,)), ((), ()))):
    return lax.dot_general(a, b, dims, preferred_element_type=F32)


PACK = EXPERTS * 8
WIDE = 1536
CHUNK = EXPERTS * CAP
HALF = D // 2
EXTRA = 16


def picked(ids, valid, places):
    ids = jnp.where(valid, ids, -1).astype(F32)
    return ones_where(jnp.logical_or(ids == places[0], ids == places[1]))


def dispatch_x_kernel(
    stream_ref, grad_ref, gain_ref, routes_ref, gates_ref, k_ref, v_ref, packed_ref, block_ref, both_ref
):
    s = stream_ref[...].astype(F32)
    inverse_rms = lax.rsqrt(jnp.mean(s * s, -1, keepdims=True) + EPSILON)
    normed = ((s * inverse_rms) * gain_ref[...]).astype(BF16)
    routes = routes_ref[...]
    expert = iota((EXPERTS, FRAMES), 0)
    named = [expert == routes[k : k + 1, :] for k in range(2)]
    count = ones_where(jnp.logical_or(named[0], named[1]))
    earlier = ones_where(iota((FRAMES, FRAMES), 0) < iota((FRAMES, FRAMES), 1))
    before = matmul(count, earlier)
    route = [routes[k : k + 1, :].astype(F32) for k in range(2)]
    slot = [jnp.sum(jnp.where(named[k], before, 0.0), 0, keepdims=True) for k in range(2)]
    places = [route[k] * CAP + slot[k] for k in range(2)]
    split = []
    for k in range(2):
        gate = gates_ref[k : k + 1, :]
        high = gate.astype(BF16).astype(F32)
        middle = (gate - high).astype(BF16).astype(F32)
        split += [high, middle, gate - high - middle]
    block_ref[0:FRAMES, :] = grad_ref[...]
    block_ref[FRAMES:, :] = jnp.zeros((EXTRA, D), BF16)
    extra = jnp.concatenate(route + slot + split + [jnp.zeros((EXTRA - 10, FRAMES), F32)], 0)
    block_ref[FRAMES:, 0:FRAMES] = extra.astype(BF16)
    both_ref[0] = k_ref[...]
    both_ref[1] = v_ref[...]
    row = iota((PACK, FRAMES), 0)
    r = row & 7
    base = (row >> 3) * CAP
    main = picked(base + r, r < 8, places)
    low = picked(base + 8 + r, r < 4, places)
    high = picked(base + 4 + r, r >= 4, places)
    packed_ref[:, 0:D] = matmul(main, normed).astype(BF16)
    packed_ref[:, D:] = (matmul(low, normed[:, :HALF]) + matmul(high, normed[:, HALF:])).astype(BF16)


def dispatch_x(stream, grad, gain, routes, gates, keys, values):
    return pl.pallas_call(
        dispatch_x_kernel,
        out_shape=(
            jax.ShapeDtypeStruct((PACK, WIDE), BF16),
            jax.ShapeDtypeStruct((FRAMES + EXTRA, D), BF16),
            jax.ShapeDtypeStruct((2, FRAMES, D), BF16),
        ),
        name="dispatch_x",
    )(stream, grad, gain, routes, gates, keys, values)


def dispatch_g_kernel(*refs):
    blocks, out_ref, pairs, keys = refs[:EP], refs[EP], refs[EP + 1], refs[EP + 2]
    step = pl.program_id(0)

    for q in range(EP):

        @pl.when(step == q)
        def _(q=q):
            extra = blocks[q][FRAMES:, 0:FRAMES].astype(F32)
            upright = extra.T
            g = blocks[q][0:FRAMES, :].astype(F32)
            for k in range(2):
                gate = upright[:, 4 + 3 * k : 5 + 3 * k] + upright[:, 5 + 3 * k : 6 + 3 * k]
                gate = gate + upright[:, 6 + 3 * k : 7 + 3 * k]
                pairs[k * FRAMES : (k + 1) * FRAMES, :] = (gate * g).astype(BF16)
                keys[k : k + 1, :] = extra[k : k + 1, :] * CAP + extra[2 + k : 3 + k, :]

    row = iota((PACK, FRAMES), 0)
    r = row & 7
    base = (row >> 3) * CAP

    def pick(ids, valid):
        ids = jnp.where(valid, ids, -1).astype(F32)
        return jnp.concatenate([ones_where(ids == keys[k : k + 1, :]) for k in range(2)], 1)

    main = pick(base + r, r < 8)
    low = pick(base + 8 + r, r < 4)
    high = pick(base + 4 + r, r >= 4)
    out_ref[:, 0, :, 0:D] = matmul(main, pairs[...]).reshape(EXPERTS, 8, D).astype(BF16)
    rest = matmul(low, pairs[:, :HALF]) + matmul(high, pairs[:, HALF:])
    out_ref[:, 0, :, D:] = rest.reshape(EXPERTS, 8, HALF).astype(BF16)


def dispatch_g(blocks):
    return pl.pallas_call(
        dispatch_g_kernel,
        grid=(EP,),
        in_specs=[VMEM_SPEC, VMEM_SPEC, pl.BlockSpec((FRAMES + EXTRA, D), lambda i: (0, 0)), VMEM_SPEC],
        out_specs=pl.BlockSpec((EXPERTS, 1, 8, WIDE), lambda i: (0, i, 0, 0)),
        out_shape=jax.ShapeDtypeStruct((EXPERTS, EP, 8, WIDE), BF16),
        scratch_shapes=[pltpu.VMEM((2 * FRAMES, D), BF16), pltpu.VMEM((8, FRAMES), F32)],
        name="dispatch_g",
    )(*blocks)


def fill_moves(moves, packed_dim):
    shape = (PACK, PACK // 2) if packed_dim == 0 else (PACK // 2, PACK)
    p = iota(shape, packed_dim)
    r = iota(shape, 1 - packed_dim)
    same = (p >> 3) == (r >> 2)
    for n in range(2):
        moves[n] = ones_where(jnp.logical_and(same, (p & 7) == (r & 3) + 4 * n))


def unpack(packed, moves, out_ref, start):
    out_ref[start : start + PACK, :] = packed[:, 0:D]
    for n in range(2):
        rest = matmul(moves[n], packed[:, D:]).astype(BF16)
        out_ref[start + PACK : start + CHUNK, n * HALF : (n + 1) * HALF] = rest


N_BLOCK = 512


def forward_kernel(count, *refs):
    parts, gate_ref, up_ref = refs[:count], refs[count], refs[count + 1]
    x_ref, a_ref, s_ref, acted_ref, moves = refs[-5:]

    @pl.when(pl.program_id(0) == 0)
    def _():
        fill_moves(moves, 1)
        for n, part in enumerate(parts):
            unpack(part[...], moves, x_ref, n * CHUNK)

    x = x_ref[...]
    gate = matmul(x, gate_ref[...])
    up = matmul(x, up_ref[...])
    sig = jax.nn.sigmoid(gate)
    silu = gate * sig
    acted_ref[...] = (silu * up).astype(BF16)
    s_ref[...] = silu
    a_ref[...] = up * sig * (1.0 + gate * (1.0 - sig))


def expert_forward(q, parts, w_gate, w_up, filled):
    rows = len(parts) * CHUNK
    whole = [VMEM_SPEC] * len(parts)
    weight = pl.BlockSpec((D, N_BLOCK), lambda j: (0, j))
    out = pl.BlockSpec((rows, N_BLOCK), lambda j: (q, j))
    shape = lambda t: jax.ShapeDtypeStruct((ROWS, D), t)
    n = len(parts)
    return pl.pallas_call(
        lambda *refs: forward_kernel(n, *refs),
        grid=(D // N_BLOCK,),
        in_specs=whole + [weight] * 2 + [pl.BlockSpec(memory_space=pl.ANY)] * len(filled),
        out_specs=[pl.BlockSpec((rows, D), lambda j: (q, 0)), out, out, out],
        out_shape=(shape(BF16), shape(F32), shape(F32), shape(BF16)),
        scratch_shapes=[pltpu.VMEM((2, PACK // 2, PACK), BF16)],
        input_output_aliases={n + 2 + i: i for i in range(len(filled))},
        name="expert_forward",
    )(*[near(p) for p in parts], w_gate, w_up, *filled)


def backward_kernel(
    column_ref, packed_ref, a_ref, s_ref, gate_ref, up_ref, down_ref, g_ref, dgate_ref, dup_ref, out_ref, moves, back
):
    @pl.when(pl.program_id(0) == 0)
    def _():
        fill_moves(moves, 1)
        fill_moves(back, 0)

    unpack(packed_ref[...].astype(F32).reshape(PACK, WIDE).astype(BF16), moves, g_ref, 0)
    dact = matmul(g_ref[...], down_ref[...], NT)
    dgate = (dact * a_ref[...]).astype(BF16)
    dup = (dact * s_ref[...]).astype(BF16)
    dgate_ref[...] = dgate
    dup_ref[...] = dup
    dx = matmul(dgate, gate_ref[...], NT) + matmul(dup, up_ref[...], NT)
    out_ref[:, 0, :, 0:D] = dx[:PACK].reshape(EXPERTS, 8, D).astype(BF16)
    last = dx[PACK:].astype(BF16)
    rest = matmul(back[0], last[:, :HALF]) + matmul(back[1], last[:, HALF:])
    out_ref[:, 0, :, D:] = rest.reshape(EXPERTS, 8, HALF).astype(BF16)


def expert_backward(column, packed, a, s, w_gate, w_up, w_down):
    def home(q, c):
        return (c[0] + jnp.where(q < 2, 3 - 2 * q, 2 * q - 4)) & 3

    weight = pl.BlockSpec((D, D), lambda i, c: (0, 0), pipeline_mode=pl.Buffered(1))
    rows = pl.BlockSpec((CHUNK, D), lambda i, c: (i, 0))
    shape = jax.ShapeDtypeStruct((ROWS, D), BF16)
    return pl.pallas_call(
        backward_kernel,
        grid_spec=pltpu.PrefetchScalarGridSpec(
            num_scalar_prefetch=1,
            grid=(EP,),
            in_specs=[
                pl.BlockSpec((EXPERTS, 1, 8, WIDE), lambda i, c: (0, i, 0, 0)),
                rows,
                rows,
                weight,
                weight,
                weight,
            ],
            out_specs=[rows, rows, rows, pl.BlockSpec((EXPERTS, 1, 8, WIDE), lambda i, c: (0, home(i, c), 0, 0))],
            scratch_shapes=[
                pltpu.VMEM((2, PACK // 2, PACK), BF16),
                pltpu.VMEM((2, PACK, PACK // 2), BF16),
            ],
        ),
        out_shape=(shape, shape, shape, jax.ShapeDtypeStruct((EXPERTS, EP, 8, WIDE), BF16)),
        name="expert_backward",
    )(column, packed, a, s, w_gate, w_up, w_down)


WINDOW = LEFT + FRAMES
SCALE = 1.0 / math.sqrt(HEAD)
PAIR = 2 * HEAD
STEP_PAIRS = 2
WIDTH = STEP_PAIRS * PAIR
STEP_HEADS = 2 * STEP_PAIRS
STEPS = HEADS // STEP_HEADS


def one_head(pair, h):
    lane = iota(pair.shape, 1)
    mask = lane >= HEAD if h else lane < HEAD
    return jnp.where(mask, pair.astype(F32), 0.0).astype(BF16)


def lanes(n):
    return slice(n * PAIR, (n + 1) * PAIR)


def columns_spec(*lead):
    return pl.BlockSpec((*lead, WIDTH), lambda i, *_: (0,) * len(lead) + (i,))


def heads_spec(*rest):
    return pl.BlockSpec((STEP_HEADS, *rest), lambda i, *_: (i,) + (0,) * len(rest))


def probs_kernel(first_ref, q_ref, both2_ref, both1_ref, k_ref, v_ref, p_ref, stats_ref, attn_ref):
    s = iota((WINDOW, FRAMES), 0)
    skipped = jnp.where(iota((WINDOW, FRAMES), 1) >= SPAN, SPAN, 0)
    allowed = jnp.logical_and(s >= skipped, s < skipped + (WINDOW - SPAN))
    allowed = jnp.logical_and(allowed, s >= first_ref[0])
    stats_ref[...] = jnp.zeros((STEP_HEADS, 8, FRAMES), F32)
    for n in range(STEP_PAIRS):
        c = lanes(n)
        keys = jnp.concatenate([both2_ref[0, :, c], both1_ref[0, :, c], k_ref[:, c]], 0)
        values = jnp.concatenate([both2_ref[1, :, c], both1_ref[1, :, c], v_ref[:, c]], 0)
        q = q_ref[:, c]
        attn = 0.0
        for h in range(2):
            at = 2 * n + h
            scores = matmul(keys, one_head(q, h), NT) * SCALE
            scores = jnp.where(allowed, scores, -jnp.inf)
            top = jnp.max(scores, 0, keepdims=True)
            e = jnp.exp(scores - top)
            inverse = 1.0 / jnp.sum(e, 0, keepdims=True)
            probs = e * inverse
            p_ref[at] = probs
            attn += matmul(probs.astype(BF16), one_head(values, h), TN)
            stats_ref[at, 0:1, :] = top
            stats_ref[at, 1:2, :] = inverse
        attn_ref[:, c] = attn


def attention_probs(first, q, both2, both1, k, v):
    both, one = columns_spec(2, FRAMES), columns_spec(FRAMES)
    return pl.pallas_call(
        probs_kernel,
        grid_spec=pltpu.PrefetchScalarGridSpec(
            num_scalar_prefetch=1,
            grid=(STEPS,),
            in_specs=[one, both, both, one, one],
            out_specs=[heads_spec(WINDOW, FRAMES), heads_spec(8, FRAMES), one],
        ),
        out_shape=(
            jax.ShapeDtypeStruct((HEADS, WINDOW, FRAMES), F32),
            jax.ShapeDtypeStruct((HEADS, 8, FRAMES), F32),
            jax.ShapeDtypeStruct((FRAMES, D), F32),
        ),
        name="attention_probs",
    )(first, q, both2, both1, k, v)


def later_probs_kernel(q1_ref, q2_ref, stats1_ref, stats2_ref, k_ref, p_ref):
    shape = (FRAMES, FRAMES)
    allowed = iota(shape, 0) >= jnp.where(iota(shape, 1) >= SPAN, SPAN, 0)
    for n in range(STEP_PAIRS):
        k = k_ref[:, lanes(n)]
        for m, (q_ref, stats_ref) in enumerate(((q1_ref, stats1_ref), (q2_ref, stats2_ref))):
            q = q_ref[:, lanes(n)]
            for h in range(2):
                at = 2 * n + h
                scores = matmul(k, one_head(q, h), NT) * SCALE
                if m == 1:
                    scores = jnp.where(allowed, scores, -jnp.inf)
                p_ref[at, m] = jnp.exp(scores - stats_ref[at, 0:1, :]) * stats_ref[at, 1:2, :]


def later_probs(q1, q2, stats1, stats2, k):
    one, stats = columns_spec(FRAMES), heads_spec(8, FRAMES)
    return pl.pallas_call(
        later_probs_kernel,
        grid=(STEPS,),
        in_specs=[one, one, stats, stats, one],
        out_specs=heads_spec(2, FRAMES, FRAMES),
        out_shape=jax.ShapeDtypeStruct((HEADS, 2, FRAMES, FRAMES), F32),
        name="later_probs",
    )(q1, q2, stats1, stats2, k)


def thirds(x):
    high = x.astype(BF16)
    rest = x - high.astype(F32)
    middle = rest.astype(BF16)
    return high, middle, (rest - middle.astype(F32)).astype(BF16)


def stream_grad_kernel(rows_ref, block_ref, stream_ref, gain_ref, attn_ref, o_ref, sent_ref, main, total):
    j = pl.program_id(0)
    upright = block_ref[FRAMES:, 0:FRAMES].astype(F32).T
    places = [upright[:, k : k + 1] * CAP + upright[:, 2 + k : 3 + k] for k in range(2)]
    row = iota((FRAMES, PACK * EP), 1)
    r = row & 7
    base = (row >> 5) * CAP

    @pl.when(j == 0)
    def _():
        main[...] = picked(base + r, r < 8, places)

    @pl.when(j < 2)
    def _():
        total[j] = matmul(main[...], rows_ref[:, pl.ds(pl.multiple_of(j * HALF, HALF), HALF)])

    @pl.when(j == 2)
    def _():
        low = picked(base + 8 + r, r < 4, places)
        high = picked(base + 4 + r, r >= 4, places)
        rest = matmul(jnp.concatenate([low, high], 0), rows_ref[:, D:])
        dnormed = jnp.concatenate([total[0] + rest[:FRAMES], total[1] + rest[FRAMES:]], 1)
        s = stream_ref[...].astype(F32)
        inverse_rms = lax.rsqrt(jnp.mean(s * s, -1, keepdims=True) + EPSILON)
        scaled = s * inverse_rms
        weighted = dnormed * gain_ref[...]
        mean = jnp.mean(weighted * scaled, -1, keepdims=True)
        grad = block_ref[0:FRAMES, :].astype(F32)
        o = (grad + inverse_rms * (weighted - scaled * mean)).astype(BF16)
        o_ref[...] = o
        sent_ref[0:FRAMES, :] = o
        head = ones_where((iota((HEADS, D), 1) >> 6) == iota((HEADS, D), 0))
        delta = 0.0
        for part in thirds(o.astype(F32) * attn_ref[...]):
            delta += matmul(head, part, NT)
        sent_ref[FRAMES:, :] = jnp.concatenate(
            [*thirds(delta), jnp.zeros((HEADS, D - 3 * FRAMES), BF16)], 1
        )


def stream_gradient(returned, block, stream, gain, attn):
    whole = lambda n: pl.BlockSpec((n, D), lambda j: (0, 0))
    return pl.pallas_call(
        stream_grad_kernel,
        grid=(3,),
        in_specs=[
            pl.BlockSpec(memory_space=pltpu.VMEM),
            whole(FRAMES + EXTRA),
            whole(FRAMES),
            whole(1),
            whole(FRAMES),
        ],
        out_specs=[whole(FRAMES), whole(FRAMES + HEADS)],
        out_shape=(
            jax.ShapeDtypeStruct((FRAMES, D), BF16),
            jax.ShapeDtypeStruct((FRAMES + HEADS, D), BF16),
        ),
        scratch_shapes=[pltpu.VMEM((FRAMES, PACK * EP), BF16), pltpu.VMEM((2, FRAMES, HALF), F32)],
        name="stream_gradient",
    )(returned, block, stream, gain, attn)


DELTA_SPEC = pl.BlockSpec((HEADS, 3 * FRAMES), lambda i: (FRAMES // HEADS, 0))


def delta_of(ref):
    part = lambda n: ref[:, n * FRAMES : (n + 1) * FRAMES].astype(F32)
    return part(0) + part(1) + part(2)


def own_grads_kernel(
    p_ref, o_ref, extra_ref, q_ref, both2_ref, both1_ref, k_ref, v_ref, dq_ref, dk_ref, dv_ref, deltas
):
    deltas[...] = delta_of(extra_ref)
    for n in range(STEP_PAIRS):
        c = lanes(n)
        o, q = o_ref[:, c], q_ref[:, c]
        keys = jnp.concatenate([both2_ref[0, :, c], both1_ref[0, :, c], k_ref[:, c]], 0)
        values = jnp.concatenate([both2_ref[1, :, c], both1_ref[1, :, c], v_ref[:, c]], 0)
        dq = dk = dv = 0.0
        for h in range(2):
            at = 2 * n + h
            o_h, q_h, k_h = one_head(o, h), one_head(q, h), one_head(keys, h)
            probs = p_ref[at]
            delta = deltas[pl.ds(STEP_HEADS * pl.program_id(0) + at, 1), :]
            dscore = (probs * (matmul(values, o_h, NT) - delta)).astype(BF16)
            dq += matmul(dscore, k_h, TN)
            dk += matmul(dscore[LEFT:], q_h)
            dv += matmul(probs[LEFT:].astype(BF16), o_h)
        dq_ref[:, c] = (dq * SCALE).astype(BF16)
        dk_ref[:, c] = dk
        dv_ref[:, c] = dv


def own_grads(probs, sent, q, both2, both1, keys, values):
    one, both = columns_spec(FRAMES), columns_spec(2, FRAMES)
    out = lambda t: jax.ShapeDtypeStruct((FRAMES, D), t)
    return pl.pallas_call(
        own_grads_kernel,
        grid=(STEPS,),
        in_specs=[heads_spec(WINDOW, FRAMES), one, DELTA_SPEC, one, both, both, one, one],
        out_specs=[one, one, one],
        out_shape=(out(BF16), out(F32), out(F32)),
        scratch_shapes=[pltpu.VMEM((HEADS, FRAMES), F32)],
        name="own_grads",
    )(probs, sent, sent, q, both2, both1, keys, values)


def later_grads_kernel(
    p_ref, o1_ref, o2_ref, q1_ref, q2_ref, v_ref, dk_ref, dv_ref, keys_ref, values_ref, deltas
):
    deltas[0] = delta_of(o1_ref.at[FRAMES:, :])
    deltas[1] = delta_of(o2_ref.at[FRAMES:, :])
    for n in range(STEP_PAIRS):
        c = lanes(n)
        v = v_ref[:, c]
        dk, dv = dk_ref[:, c], dv_ref[:, c]
        for m, (o_ref, q_ref) in enumerate(((o1_ref, q1_ref), (o2_ref, q2_ref))):
            place = pl.multiple_of(WIDTH * pl.program_id(0) + PAIR * n, PAIR)
            o, q = o_ref[0:FRAMES, pl.ds(place, PAIR)], q_ref[:, c]
            for h in range(2):
                at = 2 * n + h
                o_h, q_h = one_head(o, h), one_head(q, h)
                probs = p_ref[at, m]
                delta = deltas[m, pl.ds(STEP_HEADS * pl.program_id(0) + at, 1), :]
                dscore = (probs * (matmul(v, o_h, NT) - delta)).astype(BF16)
                dk += matmul(dscore, q_h)
                dv += matmul(probs.astype(BF16), o_h)
        keys_ref[:, c] = (dk * SCALE).astype(BF16)
        values_ref[:, c] = dv.astype(BF16)


def later_grads(probs, os, qs, v, dk, dv):
    one = columns_spec(FRAMES)
    return pl.pallas_call(
        later_grads_kernel,
        grid=(STEPS,),
        in_specs=[heads_spec(2, FRAMES, FRAMES), VMEM_SPEC, VMEM_SPEC] + [one] * 5,
        out_specs=[one, one],
        out_shape=(jax.ShapeDtypeStruct((FRAMES, D), BF16),) * 2,
        scratch_shapes=[pltpu.VMEM((2, HEADS, FRAMES), F32)],
        name="later_grads",
    )(probs, *os, *qs, v, dk, dv)


def near(x):
    return pltpu.with_memory_space_constraint(x, pltpu.VMEM)


def turned(x, distance):
    return lax.ppermute(x, "ep", [(i, (i + distance) % EP) for i in range(EP)])


def shifted(x, distance):
    count = lax.axis_size("tm") * lax.axis_size("ep")
    route = [(i, i + distance) for i in range(count) if 0 <= i + distance < count]
    return lax.ppermute(x, ("tm", "ep"), route)


def exchanged(x, axes):
    return lax.all_to_all(x, axes, split_axis=0, concat_axis=0, tiled=True)


def step(
    queries, keys, values, stream, grad_out, norm_gain, gate_probs, routes, w_gate, w_up, w_down
):
    gain = norm_gain.reshape(1, D)
    weight_gate, weight_up, weight_down = w_gate[0], w_up[0], w_down[0]
    row, column = lax.axis_index("tm"), lax.axis_index("ep")
    packed, block, both = dispatch_x(
        stream, grad_out, gain, routes.T, gate_probs.T, keys, values
    )
    block_left = turned(block, 1)
    block_right = turned(block, -1)
    block_far = turned(block, 2)
    own = exchanged(packed.reshape(EXPERTS, 8, WIDE), "tm").reshape(PACK, WIDE)
    left = turned(own, 1)
    right = turned(own, -1)
    far = turned(left, 1)
    sent_g = dispatch_g((near(block_left), near(block_right), block, near(block_far))).reshape(EXPERTS, EP * 8, WIDE)
    packed_g = exchanged(sent_g, "tm").reshape(EXPERTS, EP, 8, WIDE)
    filled = expert_forward(2, (own,), weight_gate, weight_up, ())
    filled = expert_forward(0, (left, right), weight_gate, weight_up, filled)
    x_rows, a, s, acted = expert_forward(3, (far,), weight_gate, weight_up, filled)
    both1 = shifted(both, 1)
    both2 = shifted(both, 2)
    q1 = shifted(queries, -1)
    q2 = shifted(queries, -2)
    g_rows, dgate, dup, dx = expert_backward(
        column.astype(jnp.int32).reshape(1), packed_g, a, s, weight_gate, weight_up, weight_down
    )
    returned = exchanged(dx.reshape(EXPERTS * EP, 8, WIDE), ("tm", "ep")).reshape(PACK * EP, WIDE)
    gate_grad = jnp.dot(x_rows.T, dgate, preferred_element_type=F32)
    up_grad = jnp.dot(x_rows.T, dup, preferred_element_type=F32)
    down_grad = jnp.dot(acted.T, g_rows, preferred_element_type=F32)
    position = row * lax.axis_size("ep") + column
    first = jnp.maximum(LEFT - position * FRAMES, 0).astype(jnp.int32).reshape(1)
    probs, stats, attn = attention_probs(first, queries, both2, both1, keys, values)
    stats1 = shifted(stats, -1)
    stats2 = shifted(stats, -2)
    later = later_probs(q1, q2, stats1, stats2, keys)
    returned, probs, gate_grad, up_grad, down_grad = lax.optimization_barrier(
        (returned, probs, gate_grad, up_grad, down_grad)
    )
    stream_grad, sent_o = stream_gradient(near(returned), block, stream, gain, attn)
    o1 = shifted(sent_o, -1)
    o2 = shifted(sent_o, -2)
    grad_q, own_k, own_v = own_grads(probs, sent_o, queries, both2, both1, keys, values)
    grad_k, grad_v = later_grads(later, (near(o1), near(o2)), (q1, q2), values, own_k, own_v)
    return (
        grad_q,
        grad_k,
        grad_v,
        stream_grad,
        gate_grad[None],
        up_grad[None],
        down_grad[None],
    )


def solution(mesh):
    frames = P(("tm", "ep"), None)
    columns, rows = P("tm", None, "ep"), P("tm", "ep", None)
    return jax.shard_map(
        step,
        mesh=mesh,
        in_specs=(frames,) * 5 + (P(), frames, frames, columns, columns, rows),
        out_specs=(frames,) * 4 + (columns, columns, rows),
        check_vma=False,
    )
```

```python
import math

import jax
import jax.numpy as jnp
from jax import lax
from jax.experimental import pallas as pl
from jax.experimental.pallas import tpu as pltpu
from jax.sharding import PartitionSpec as P


D = 1024
HEADS = 16
HEAD = 64
SPAN = 64
LEFT = 256
FRAMES = 128
EXPERTS = 32
CAP = 12
EP = 4
ROWS = EXPERTS * EP * CAP
EPSILON = 1e-06
BF16 = jnp.bfloat16
F32 = jnp.float32
NT = (((1,), (1,)), ((), ()))
TN = (((0,), (0,)), ((), ()))


VMEM_SPEC = pl.BlockSpec(memory_space=pltpu.VMEM)


def iota(shape, dim):
    return lax.broadcasted_iota(jnp.int32, shape, dim)


def ones_where(mask):
    return jnp.where(mask, 1.0, 0.0).astype(BF16)


def matmul(a, b, dims=(((1,), (0,)), ((), ()))):
    return lax.dot_general(a, b, dims, preferred_element_type=F32)


PACK = EXPERTS * 8
WIDE = 1536
CHUNK = EXPERTS * CAP
HALF = D // 2
EXTRA = 16


def picked(ids, valid, places):
    ids = jnp.where(valid, ids, -1).astype(F32)
    return ones_where(jnp.logical_or(ids == places[0], ids == places[1]))


def dispatch_x_kernel(
    stream_ref, grad_ref, gain_ref, routes_ref, gates_ref, k_ref, v_ref, packed_ref, block_ref, both_ref
):
    s = stream_ref[...].astype(F32)
    inverse_rms = lax.rsqrt(jnp.mean(s * s, -1, keepdims=True) + EPSILON)
    normed = ((s * inverse_rms) * gain_ref[...]).astype(BF16)
    routes = routes_ref[...]
    expert = iota((EXPERTS, FRAMES), 0)
    named = [expert == routes[k : k + 1, :] for k in range(2)]
    count = ones_where(jnp.logical_or(named[0], named[1]))
    earlier = ones_where(iota((FRAMES, FRAMES), 0) < iota((FRAMES, FRAMES), 1))
    before = matmul(count, earlier)
    route = [routes[k : k + 1, :].astype(F32) for k in range(2)]
    slot = [jnp.sum(jnp.where(named[k], before, 0.0), 0, keepdims=True) for k in range(2)]
    places = [route[k] * CAP + slot[k] for k in range(2)]
    split = []
    for k in range(2):
        gate = gates_ref[k : k + 1, :]
        high = gate.astype(BF16).astype(F32)
        middle = (gate - high).astype(BF16).astype(F32)
        split += [high, middle, gate - high - middle]
    block_ref[0:FRAMES, :] = grad_ref[...]
    block_ref[FRAMES:, :] = jnp.zeros((EXTRA, D), BF16)
    extra = jnp.concatenate(route + slot + split + [jnp.zeros((EXTRA - 10, FRAMES), F32)], 0)
    block_ref[FRAMES:, 0:FRAMES] = extra.astype(BF16)
    both_ref[0] = k_ref[...]
    both_ref[1] = v_ref[...]
    row = iota((PACK, FRAMES), 0)
    r = row & 7
    base = (row >> 3) * CAP
    main = picked(base + r, r < 8, places)
    low = picked(base + 8 + r, r < 4, places)
    high = picked(base + 4 + r, r >= 4, places)
    packed_ref[:, 0:D] = matmul(main, normed).astype(BF16)
    packed_ref[:, D:] = (matmul(low, normed[:, :HALF]) + matmul(high, normed[:, HALF:])).astype(BF16)


def dispatch_x(stream, grad, gain, routes, gates, keys, values):
    return pl.pallas_call(
        dispatch_x_kernel,
        out_shape=(
            jax.ShapeDtypeStruct((PACK, WIDE), BF16),
            jax.ShapeDtypeStruct((FRAMES + EXTRA, D), BF16),
            jax.ShapeDtypeStruct((2, FRAMES, D), BF16),
        ),
        name="dispatch_x",
    )(stream, grad, gain, routes, gates, keys, values)


def dispatch_g_kernel(*refs):
    blocks, out_ref, pairs, keys = refs[:EP], refs[EP], refs[EP + 1], refs[EP + 2]
    step = pl.program_id(0)

    for q in range(EP):

        @pl.when(step == q)
        def _(q=q):
            extra = blocks[q][FRAMES:, 0:FRAMES].astype(F32)
            upright = extra.T
            g = blocks[q][0:FRAMES, :].astype(F32)
            for k in range(2):
                gate = upright[:, 4 + 3 * k : 5 + 3 * k] + upright[:, 5 + 3 * k : 6 + 3 * k]
                gate = gate + upright[:, 6 + 3 * k : 7 + 3 * k]
                pairs[k * FRAMES : (k + 1) * FRAMES, :] = (gate * g).astype(BF16)
                keys[k : k + 1, :] = extra[k : k + 1, :] * CAP + extra[2 + k : 3 + k, :]

    row = iota((PACK, FRAMES), 0)
    r = row & 7
    base = (row >> 3) * CAP

    def pick(ids, valid):
        ids = jnp.where(valid, ids, -1).astype(F32)
        return jnp.concatenate([ones_where(ids == keys[k : k + 1, :]) for k in range(2)], 1)

    main = pick(base + r, r < 8)
    low = pick(base + 8 + r, r < 4)
    high = pick(base + 4 + r, r >= 4)
    out_ref[:, 0, :, 0:D] = matmul(main, pairs[...]).reshape(EXPERTS, 8, D).astype(BF16)
    rest = matmul(low, pairs[:, :HALF]) + matmul(high, pairs[:, HALF:])
    out_ref[:, 0, :, D:] = rest.reshape(EXPERTS, 8, HALF).astype(BF16)


def dispatch_g(blocks):
    return pl.pallas_call(
        dispatch_g_kernel,
        grid=(EP,),
        in_specs=[VMEM_SPEC, VMEM_SPEC, pl.BlockSpec((FRAMES + EXTRA, D), lambda i: (0, 0)), VMEM_SPEC],
        out_specs=pl.BlockSpec((EXPERTS, 1, 8, WIDE), lambda i: (0, i, 0, 0)),
        out_shape=jax.ShapeDtypeStruct((EXPERTS, EP, 8, WIDE), BF16),
        scratch_shapes=[pltpu.VMEM((2 * FRAMES, D), BF16), pltpu.VMEM((8, FRAMES), F32)],
        name="dispatch_g",
    )(*blocks)


def fill_moves(moves, packed_dim):
    shape = (PACK, PACK // 2) if packed_dim == 0 else (PACK // 2, PACK)
    p = iota(shape, packed_dim)
    r = iota(shape, 1 - packed_dim)
    same = (p >> 3) == (r >> 2)
    for n in range(2):
        moves[n] = ones_where(jnp.logical_and(same, (p & 7) == (r & 3) + 4 * n))


def unpack(packed, moves, out_ref, start):
    out_ref[start : start + PACK, :] = packed[:, 0:D]
    for n in range(2):
        rest = matmul(moves[n], packed[:, D:]).astype(BF16)
        out_ref[start + PACK : start + CHUNK, n * HALF : (n + 1) * HALF] = rest


N_BLOCK = 512


def forward_kernel(count, *refs):
    parts, gate_ref, up_ref = refs[:count], refs[count], refs[count + 1]
    x_ref, a_ref, s_ref, acted_ref, moves = refs[-5:]

    @pl.when(pl.program_id(0) == 0)
    def _():
        fill_moves(moves, 1)
        for n, part in enumerate(parts):
            unpack(part[...], moves, x_ref, n * CHUNK)

    x = x_ref[...]
    gate = matmul(x, gate_ref[...])
    up = matmul(x, up_ref[...])
    sig = jax.nn.sigmoid(gate)
    silu = gate * sig
    acted_ref[...] = (silu * up).astype(BF16)
    s_ref[...] = silu
    a_ref[...] = up * sig * (1.0 + gate * (1.0 - sig))


def expert_forward(q, parts, w_gate, w_up, filled):
    rows = len(parts) * CHUNK
    whole = [VMEM_SPEC] * len(parts)
    weight = pl.BlockSpec((D, N_BLOCK), lambda j: (0, j))
    out = pl.BlockSpec((rows, N_BLOCK), lambda j: (q, j))
    shape = lambda t: jax.ShapeDtypeStruct((ROWS, D), t)
    n = len(parts)
    return pl.pallas_call(
        lambda *refs: forward_kernel(n, *refs),
        grid=(D // N_BLOCK,),
        in_specs=whole + [weight] * 2 + [pl.BlockSpec(memory_space=pl.ANY)] * len(filled),
        out_specs=[pl.BlockSpec((rows, D), lambda j: (q, 0)), out, out, out],
        out_shape=(shape(BF16), shape(F32), shape(F32), shape(BF16)),
        scratch_shapes=[pltpu.VMEM((2, PACK // 2, PACK), BF16)],
        input_output_aliases={n + 2 + i: i for i in range(len(filled))},
        name="expert_forward",
    )(*[near(p) for p in parts], w_gate, w_up, *filled)


def backward_kernel(
    column_ref, packed_ref, a_ref, s_ref, gate_ref, up_ref, down_ref, g_ref, dgate_ref, dup_ref, out_ref, moves, back
):
    @pl.when(pl.program_id(0) == 0)
    def _():
        fill_moves(moves, 1)
        fill_moves(back, 0)

    unpack(packed_ref[...].astype(F32).reshape(PACK, WIDE).astype(BF16), moves, g_ref, 0)
    dact = matmul(g_ref[...], down_ref[...], NT)
    dgate = (dact * a_ref[...]).astype(BF16)
    dup = (dact * s_ref[...]).astype(BF16)
    dgate_ref[...] = dgate
    dup_ref[...] = dup
    dx = matmul(dgate, gate_ref[...], NT) + matmul(dup, up_ref[...], NT)
    out_ref[:, 0, :, 0:D] = dx[:PACK].reshape(EXPERTS, 8, D).astype(BF16)
    last = dx[PACK:].astype(BF16)
    rest = matmul(back[0], last[:, :HALF]) + matmul(back[1], last[:, HALF:])
    out_ref[:, 0, :, D:] = rest.reshape(EXPERTS, 8, HALF).astype(BF16)


def expert_backward(column, packed, a, s, w_gate, w_up, w_down):
    def home(q, c):
        return (c[0] + jnp.where(q < 2, 3 - 2 * q, 2 * q - 4)) & 3

    weight = pl.BlockSpec((D, D), lambda i, c: (0, 0), pipeline_mode=pl.Buffered(1))
    rows = pl.BlockSpec((CHUNK, D), lambda i, c: (i, 0))
    shape = jax.ShapeDtypeStruct((ROWS, D), BF16)
    return pl.pallas_call(
        backward_kernel,
        grid_spec=pltpu.PrefetchScalarGridSpec(
            num_scalar_prefetch=1,
            grid=(EP,),
            in_specs=[
                pl.BlockSpec((EXPERTS, 1, 8, WIDE), lambda i, c: (0, i, 0, 0)),
                rows,
                rows,
                weight,
                weight,
                weight,
            ],
            out_specs=[rows, rows, rows, pl.BlockSpec((EXPERTS, 1, 8, WIDE), lambda i, c: (0, home(i, c), 0, 0))],
            scratch_shapes=[
                pltpu.VMEM((2, PACK // 2, PACK), BF16),
                pltpu.VMEM((2, PACK, PACK // 2), BF16),
            ],
        ),
        out_shape=(shape, shape, shape, jax.ShapeDtypeStruct((EXPERTS, EP, 8, WIDE), BF16)),
        name="expert_backward",
    )(column, packed, a, s, w_gate, w_up, w_down)


WINDOW = LEFT + FRAMES
SCALE = 1.0 / math.sqrt(HEAD)
PAIR = 2 * HEAD
STEP_PAIRS = 2
WIDTH = STEP_PAIRS * PAIR
STEP_HEADS = 2 * STEP_PAIRS
STEPS = HEADS // STEP_HEADS


def one_head(pair, h):
    lane = iota(pair.shape, 1)
    mask = lane >= HEAD if h else lane < HEAD
    return jnp.where(mask, pair.astype(F32), 0.0).astype(BF16)


def lanes(n):
    return slice(n * PAIR, (n + 1) * PAIR)


def columns_spec(*lead):
    return pl.BlockSpec((*lead, WIDTH), lambda i, *_: (0,) * len(lead) + (i,))


def heads_spec(*rest):
    return pl.BlockSpec((STEP_HEADS, *rest), lambda i, *_: (i,) + (0,) * len(rest))


def probs_kernel(first_ref, q_ref, both2_ref, both1_ref, k_ref, v_ref, p_ref, stats_ref, attn_ref):
    s = iota((WINDOW, FRAMES), 0)
    skipped = jnp.where(iota((WINDOW, FRAMES), 1) >= SPAN, SPAN, 0)
    allowed = jnp.logical_and(s >= skipped, s < skipped + (WINDOW - SPAN))
    allowed = jnp.logical_and(allowed, s >= first_ref[0])
    stats_ref[...] = jnp.zeros((STEP_HEADS, 8, FRAMES), F32)
    for n in range(STEP_PAIRS):
        c = lanes(n)
        keys = jnp.concatenate([both2_ref[0, :, c], both1_ref[0, :, c], k_ref[:, c]], 0)
        values = jnp.concatenate([both2_ref[1, :, c], both1_ref[1, :, c], v_ref[:, c]], 0)
        q = q_ref[:, c]
        attn = 0.0
        for h in range(2):
            at = 2 * n + h
            scores = matmul(keys, one_head(q, h), NT) * SCALE
            scores = jnp.where(allowed, scores, -jnp.inf)
            top = jnp.max(scores, 0, keepdims=True)
            e = jnp.exp(scores - top)
            inverse = 1.0 / jnp.sum(e, 0, keepdims=True)
            probs = e * inverse
            p_ref[at] = probs
            attn += matmul(probs.astype(BF16), one_head(values, h), TN)
            stats_ref[at, 0:1, :] = top
            stats_ref[at, 1:2, :] = inverse
        attn_ref[:, c] = attn


def attention_probs(first, q, both2, both1, k, v):
    both, one = columns_spec(2, FRAMES), columns_spec(FRAMES)
    return pl.pallas_call(
        probs_kernel,
        grid_spec=pltpu.PrefetchScalarGridSpec(
            num_scalar_prefetch=1,
            grid=(STEPS,),
            in_specs=[one, both, both, one, one],
            out_specs=[heads_spec(WINDOW, FRAMES), heads_spec(8, FRAMES), one],
        ),
        out_shape=(
            jax.ShapeDtypeStruct((HEADS, WINDOW, FRAMES), F32),
            jax.ShapeDtypeStruct((HEADS, 8, FRAMES), F32),
            jax.ShapeDtypeStruct((FRAMES, D), F32),
        ),
        name="attention_probs",
    )(first, q, both2, both1, k, v)


def later_probs_kernel(q1_ref, q2_ref, stats1_ref, stats2_ref, k_ref, p_ref):
    start = STEP_HEADS * pl.program_id(0)
    shape = (FRAMES, FRAMES)
    allowed = iota(shape, 0) >= jnp.where(iota(shape, 1) >= SPAN, SPAN, 0)
    for n in range(STEP_PAIRS):
        k = k_ref[:, lanes(n)]
        for m, (q_ref, stats_ref) in enumerate(((q1_ref, stats1_ref), (q2_ref, stats2_ref))):
            q = q_ref[:, lanes(n)]
            for h in range(2):
                at = 2 * n + h
                scores = matmul(k, one_head(q, h), NT) * SCALE
                if m == 1:
                    scores = jnp.where(allowed, scores, -jnp.inf)
                p_ref[at, m] = jnp.exp(scores - stats_ref[start + at, 0:1, :]) * stats_ref[start + at, 1:2, :]


def later_probs(q1, q2, stats1, stats2, k):
    one = columns_spec(FRAMES)
    return pl.pallas_call(
        later_probs_kernel,
        grid=(STEPS,),
        in_specs=[one, one, VMEM_SPEC, VMEM_SPEC, one],
        out_specs=heads_spec(2, FRAMES, FRAMES),
        out_shape=jax.ShapeDtypeStruct((HEADS, 2, FRAMES, FRAMES), F32),
        name="later_probs",
    )(q1, q2, stats1, stats2, k)


def thirds(x):
    high = x.astype(BF16)
    rest = x - high.astype(F32)
    middle = rest.astype(BF16)
    return high, middle, (rest - middle.astype(F32)).astype(BF16)


def stream_grad_kernel(rows_ref, block_ref, stream_ref, gain_ref, attn_ref, o_ref, sent_ref, main, total):
    j = pl.program_id(0)
    upright = block_ref[FRAMES:, 0:FRAMES].astype(F32).T
    places = [upright[:, k : k + 1] * CAP + upright[:, 2 + k : 3 + k] for k in range(2)]
    row = iota((FRAMES, PACK * EP), 1)
    r = row & 7
    base = (row >> 5) * CAP

    @pl.when(j == 0)
    def _():
        main[...] = picked(base + r, r < 8, places)

    @pl.when(j < 2)
    def _():
        total[j] = matmul(main[...], rows_ref[:, pl.ds(pl.multiple_of(j * HALF, HALF), HALF)])

    @pl.when(j == 2)
    def _():
        low = picked(base + 8 + r, r < 4, places)
        high = picked(base + 4 + r, r >= 4, places)
        rest = matmul(jnp.concatenate([low, high], 0), rows_ref[:, D:])
        dnormed = jnp.concatenate([total[0] + rest[:FRAMES], total[1] + rest[FRAMES:]], 1)
        s = stream_ref[...].astype(F32)
        inverse_rms = lax.rsqrt(jnp.mean(s * s, -1, keepdims=True) + EPSILON)
        scaled = s * inverse_rms
        weighted = dnormed * gain_ref[...]
        mean = jnp.mean(weighted * scaled, -1, keepdims=True)
        grad = block_ref[0:FRAMES, :].astype(F32)
        o = (grad + inverse_rms * (weighted - scaled * mean)).astype(BF16)
        o_ref[...] = o
        sent_ref[0:FRAMES, :] = o
        head = ones_where((iota((HEADS, D), 1) >> 6) == iota((HEADS, D), 0))
        delta = 0.0
        for part in thirds(o.astype(F32) * attn_ref[...]):
            delta += matmul(head, part, NT)
        sent_ref[FRAMES:, :] = jnp.concatenate(
            [*thirds(delta), jnp.zeros((HEADS, D - 3 * FRAMES), BF16)], 1
        )


def stream_gradient(returned, block, stream, gain, attn):
    whole = lambda n: pl.BlockSpec((n, D), lambda j: (0, 0))
    return pl.pallas_call(
        stream_grad_kernel,
        grid=(3,),
        in_specs=[
            pl.BlockSpec(memory_space=pltpu.VMEM),
            whole(FRAMES + EXTRA),
            whole(FRAMES),
            whole(1),
            whole(FRAMES),
        ],
        out_specs=[whole(FRAMES), whole(FRAMES + HEADS)],
        out_shape=(
            jax.ShapeDtypeStruct((FRAMES, D), BF16),
            jax.ShapeDtypeStruct((FRAMES + HEADS, D), BF16),
        ),
        scratch_shapes=[pltpu.VMEM((FRAMES, PACK * EP), BF16), pltpu.VMEM((2, FRAMES, HALF), F32)],
        name="stream_gradient",
    )(returned, block, stream, gain, attn)


DELTA_SPEC = pl.BlockSpec((HEADS, 3 * FRAMES), lambda i: (FRAMES // HEADS, 0))


def delta_of(ref):
    part = lambda n: ref[:, n * FRAMES : (n + 1) * FRAMES].astype(F32)
    return part(0) + part(1) + part(2)


def own_grads_kernel(
    p_ref, o_ref, extra_ref, q_ref, both2_ref, both1_ref, k_ref, v_ref, dq_ref, dk_ref, dv_ref, deltas
):
    deltas[...] = delta_of(extra_ref)
    for n in range(STEP_PAIRS):
        c = lanes(n)
        o, q = o_ref[:, c], q_ref[:, c]
        keys = jnp.concatenate([both2_ref[0, :, c], both1_ref[0, :, c], k_ref[:, c]], 0)
        values = jnp.concatenate([both2_ref[1, :, c], both1_ref[1, :, c], v_ref[:, c]], 0)
        dq = dk = dv = 0.0
        for h in range(2):
            at = 2 * n + h
            o_h, q_h, k_h = one_head(o, h), one_head(q, h), one_head(keys, h)
            probs = p_ref[at]
            delta = deltas[pl.ds(STEP_HEADS * pl.program_id(0) + at, 1), :]
            dscore = (probs * (matmul(values, o_h, NT) - delta)).astype(BF16)
            dq += matmul(dscore, k_h, TN)
            dk += matmul(dscore[LEFT:], q_h)
            dv += matmul(probs[LEFT:].astype(BF16), o_h)
        dq_ref[:, c] = (dq * SCALE).astype(BF16)
        dk_ref[:, c] = dk
        dv_ref[:, c] = dv


def own_grads(probs, sent, q, both2, both1, keys, values):
    one, both = columns_spec(FRAMES), columns_spec(2, FRAMES)
    out = lambda t: jax.ShapeDtypeStruct((FRAMES, D), t)
    return pl.pallas_call(
        own_grads_kernel,
        grid=(STEPS,),
        in_specs=[heads_spec(WINDOW, FRAMES), one, DELTA_SPEC, one, both, both, one, one],
        out_specs=[one, one, one],
        out_shape=(out(BF16), out(F32), out(F32)),
        scratch_shapes=[pltpu.VMEM((HEADS, FRAMES), F32)],
        name="own_grads",
    )(probs, sent, sent, q, both2, both1, keys, values)


def later_grads_kernel(
    p_ref, o1_ref, o2_ref, q1_ref, q2_ref, v_ref, dk_ref, dv_ref, keys_ref, values_ref, deltas
):
    deltas[0] = delta_of(o1_ref.at[FRAMES:, :])
    deltas[1] = delta_of(o2_ref.at[FRAMES:, :])
    for n in range(STEP_PAIRS):
        c = lanes(n)
        v = v_ref[:, c]
        dk, dv = dk_ref[:, c], dv_ref[:, c]
        for m, (o_ref, q_ref) in enumerate(((o1_ref, q1_ref), (o2_ref, q2_ref))):
            place = pl.multiple_of(WIDTH * pl.program_id(0) + PAIR * n, PAIR)
            o, q = o_ref[0:FRAMES, pl.ds(place, PAIR)], q_ref[:, c]
            for h in range(2):
                at = 2 * n + h
                o_h, q_h = one_head(o, h), one_head(q, h)
                probs = p_ref[at, m]
                delta = deltas[m, pl.ds(STEP_HEADS * pl.program_id(0) + at, 1), :]
                dscore = (probs * (matmul(v, o_h, NT) - delta)).astype(BF16)
                dk += matmul(dscore, q_h)
                dv += matmul(probs.astype(BF16), o_h)
        keys_ref[:, c] = (dk * SCALE).astype(BF16)
        values_ref[:, c] = dv.astype(BF16)


def later_grads(probs, os, qs, v, dk, dv):
    one = columns_spec(FRAMES)
    return pl.pallas_call(
        later_grads_kernel,
        grid=(STEPS,),
        in_specs=[heads_spec(2, FRAMES, FRAMES), VMEM_SPEC, VMEM_SPEC] + [one] * 5,
        out_specs=[one, one],
        out_shape=(jax.ShapeDtypeStruct((FRAMES, D), BF16),) * 2,
        scratch_shapes=[pltpu.VMEM((2, HEADS, FRAMES), F32)],
        name="later_grads",
    )(probs, *os, *qs, v, dk, dv)


def near(x):
    return pltpu.with_memory_space_constraint(x, pltpu.VMEM)


def turned(x, distance):
    return lax.ppermute(x, "ep", [(i, (i + distance) % EP) for i in range(EP)])


def shifted(x, distance):
    count = lax.axis_size("tm") * lax.axis_size("ep")
    route = [(i, i + distance) for i in range(count) if 0 <= i + distance < count]
    return lax.ppermute(x, ("tm", "ep"), route)


def exchanged(x, axes):
    return lax.all_to_all(x, axes, split_axis=0, concat_axis=0, tiled=True)


def step(
    queries, keys, values, stream, grad_out, norm_gain, gate_probs, routes, w_gate, w_up, w_down
):
    gain = norm_gain.reshape(1, D)
    weight_gate, weight_up, weight_down = w_gate[0], w_up[0], w_down[0]
    row, column = lax.axis_index("tm"), lax.axis_index("ep")
    packed, block, both = dispatch_x(
        stream, grad_out, gain, routes.T, gate_probs.T, keys, values
    )
    block_left = turned(block, 1)
    block_right = turned(block, -1)
    block_far = turned(block, 2)
    own = exchanged(packed.reshape(EXPERTS, 8, WIDE), "tm").reshape(PACK, WIDE)
    left = turned(own, 1)
    right = turned(own, -1)
    far = turned(left, 1)
    sent_g = dispatch_g((near(block_left), near(block_right), block, near(block_far))).reshape(EXPERTS, EP * 8, WIDE)
    packed_g = exchanged(sent_g, "tm").reshape(EXPERTS, EP, 8, WIDE)
    filled = expert_forward(2, (own,), weight_gate, weight_up, ())
    filled = expert_forward(0, (left, right), weight_gate, weight_up, filled)
    x_rows, a, s, acted = expert_forward(3, (far,), weight_gate, weight_up, filled)
    both1 = shifted(both, 1)
    both2 = shifted(both, 2)
    q1 = shifted(queries, -1)
    q2 = shifted(queries, -2)
    g_rows, dgate, dup, dx = expert_backward(
        column.astype(jnp.int32).reshape(1), packed_g, a, s, weight_gate, weight_up, weight_down
    )
    returned = exchanged(dx.reshape(EXPERTS * EP, 8, WIDE), ("tm", "ep")).reshape(PACK * EP, WIDE)
    gate_grad = jnp.dot(x_rows.T, dgate, preferred_element_type=F32)
    up_grad = jnp.dot(x_rows.T, dup, preferred_element_type=F32)
    down_grad = jnp.dot(acted.T, g_rows, preferred_element_type=F32)
    position = row * lax.axis_size("ep") + column
    first = jnp.maximum(LEFT - position * FRAMES, 0).astype(jnp.int32).reshape(1)
    probs, stats, attn = attention_probs(first, queries, both2, both1, keys, values)
    stats1 = shifted(stats, -1)
    stats2 = shifted(stats, -2)
    later = later_probs(q1, q2, near(stats1), near(stats2), keys)
    returned, probs, gate_grad, up_grad, down_grad = lax.optimization_barrier(
        (returned, probs, gate_grad, up_grad, down_grad)
    )
    stream_grad, sent_o = stream_gradient(near(returned), block, stream, gain, attn)
    o1 = shifted(sent_o, -1)
    o2 = shifted(sent_o, -2)
    grad_q, own_k, own_v = own_grads(probs, sent_o, queries, both2, both1, keys, values)
    grad_k, grad_v = later_grads(later, (near(o1), near(o2)), (q1, q2), values, own_k, own_v)
    return (
        grad_q,
        grad_k,
        grad_v,
        stream_grad,
        gate_grad[None],
        up_grad[None],
        down_grad[None],
    )


def solution(mesh):
    frames = P(("tm", "ep"), None)
    columns, rows = P("tm", None, "ep"), P("tm", "ep", None)
    return jax.shard_map(
        step,
        mesh=mesh,
        in_specs=(frames,) * 5 + (P(), frames, frames, columns, columns, rows),
        out_specs=(frames,) * 4 + (columns, columns, rows),
        check_vma=False,
    )
```
